512 devices in a mesh: grp: 16 (over z, core), hap: 32 (over x, y).
Axes of the slice: x: 4, y: 8, z: 8, core: 2. Of those that a mesh axis runs over, the one named last changes fastest.
Arguments:
- alleles: int32 [240, 512], P('grp', 'hap'), may hold values from 0 to 1073741823
- observed: int32 [240, 128], P('grp', 'hap'), may hold values from 0 to 2
- map_steps: int32 [240], P('grp'), may hold values from 1 to 99
- start_weights: float32 [128, 15360], P('hap'), may hold values from 1e-12 to 1
- end_weights: float32 [128, 15360], P('hap'), may hold values from 1e-12 to 1
Outputs:
- dosage: float32 [240, 128], P('grp', 'hap')
The draws below stay inside these ranges and needn't reach their ends.
Inputs may be any that keep to these rules, and one draw needn't show every extreme that they name: Bit b of alleles[m, w] is the allele 0 or 1 of reference haplotype 30 w + b at marker m. 0 and 1 are observed alleles, 2 marks a marker not typed in that target.
All inputs are finite; a program needn't handle non-finite values.
Results may differ from the reference program's by a relative error of at most 0.0008.
Values sent between devices are 32-bit elements; how exact they have to be, the bound alone decides.
No kernel may reach another device: no remote copies, remote signals or barrier semaphores. Data moves between devices by JAX's collectives and lax.ppermute only.
A program may use at most 128 MiB of HBM per device.

```python
import math
import jax
import jax.numpy as jnp
from jax import lax

K = 15360
TGT_DEV = 4
WORDS = 512
MARKERS = 240
TARGETS = 128


def place_ends(entries, own_key, smallest, top_value):
    spot = [jax.random.randint(jax.random.fold_in(own_key, axis), (), 0, length) for axis, length in enumerate(entries.shape)]
    longest = entries.shape.index(max(entries.shape))
    next_to = spot[:longest] + [(spot[longest] + 1) % entries.shape[longest]] + spot[longest + 1:]
    return entries.at[tuple(spot)].set(smallest).at[tuple(next_to)].set(top_value)


def block_levels(rng, extent, pieces, smallest, top_value):
    level = 1.0
    for axis_at, parts in pieces:
        heights = jax.random.uniform(jax.random.fold_in(jax.random.fold_in(rng, 6), axis_at), (parts,), jnp.float32, smallest / len(pieces), top_value / len(pieces))
        level = level * jnp.repeat(jnp.exp(heights), extent[axis_at] // parts).reshape((-1,) + (1,) * (len(extent) - 1 - axis_at))
    return level


def setup_inputs(seed: int = 0) -> dict:
    key_of = jax.random.split(jax.random.key(seed), 6)
    return {
        "alleles": place_ends(jax.random.randint(key_of[0], (MARKERS, WORDS), 0, 1073741824), jax.random.fold_in(key_of[0], 1), 0, 1073741823).astype(jnp.int32),
        "observed": place_ends(jax.random.randint(key_of[1], (MARKERS, TARGETS), 0, 3), jax.random.fold_in(key_of[1], 1), 0, 2).astype(jnp.int32),
        "map_steps": place_ends(jax.random.randint(key_of[2], (MARKERS,), 1, 100), jax.random.fold_in(key_of[2], 1), 1, 99).astype(jnp.int32),
        "start_weights": jnp.clip(jnp.exp(math.log(1.0) - 27.631021 * jax.random.uniform(key_of[3], (TARGETS, K), jnp.float32) ** block_levels(key_of[3], (TARGETS, K), ((0, 32),), -0.2, 0.2)), 9.999999960041972e-13, 1.0),
        "end_weights": jnp.clip(jnp.exp(math.log(1.0) - 27.631021 * jax.random.uniform(key_of[4], (TARGETS, K), jnp.float32) ** block_levels(key_of[4], (TARGETS, K), ((0, 32),), -0.2, 0.2)), 9.999999960041972e-13, 1.0),
    }


error_rate = 0.01
map_unit = 100000.0


def unpack_alleles(packed):
    shifts = jnp.arange(30, dtype=jnp.int32)
    bits = jnp.bitwise_and(jnp.right_shift(packed[:, :, None], shifts[None, None, :]), 1)
    return bits.reshape(packed.shape[0], packed.shape[1] * 30).astype(jnp.float32)


def emission(allele_row, observed_col):
    missing = (observed_col == 2).astype(jnp.float32)[:, None]
    called = observed_col.astype(jnp.float32)[:, None]
    agree = allele_row[None, :] * called + (1.0 - allele_row[None, :]) * (1.0 - called)
    return missing + (1.0 - missing) * (error_rate + (1.0 - 2.0 * error_rate) * agree)


def forward_pass(state, haplos, observed, rates):
    total_haps = haplos.shape[1]

    def advance(carry, inputs):
        allele_row, observed_col, rate = inputs
        mixed = (1.0 - rate) * carry + (rate / total_haps) * jnp.sum(carry, axis=1, keepdims=True)
        weighted = emission(allele_row, observed_col) * mixed
        weighted = weighted / jnp.sum(weighted, axis=1, keepdims=True)
        return weighted, weighted.astype(jnp.bfloat16)

    return lax.scan(advance, state, (haplos, observed, rates))


def backward_pass(state, haplos, observed, rates):
    total_haps = haplos.shape[1]

    def retreat(carry, inputs):
        allele_row, observed_col, rate = inputs
        kept = carry.astype(jnp.bfloat16)
        weighted = emission(allele_row, observed_col) * carry
        mixed = (1.0 - rate) * weighted + (rate / total_haps) * jnp.sum(weighted, axis=1, keepdims=True)
        mixed = mixed / jnp.sum(mixed, axis=1, keepdims=True)
        return mixed, kept

    return lax.scan(retreat, state, (haplos, observed, rates), reverse=True)


def reference(alleles, observed, map_steps, start_weights, end_weights):
    haplos = unpack_alleles(alleles)
    rates = 1.0 - jnp.exp(-map_steps.astype(jnp.float32) / map_unit)
    start_rows = start_weights / jnp.sum(start_weights, axis=1, keepdims=True)
    end_rows = end_weights / jnp.sum(end_weights, axis=1, keepdims=True)
    blocks = TARGETS // TGT_DEV
    observed_blocks = observed.reshape(MARKERS, blocks, TGT_DEV).transpose(1, 0, 2)
    start_blocks = start_rows.reshape(blocks, TGT_DEV, K)
    end_blocks = end_rows.reshape(blocks, TGT_DEV, K)
    allele_half = haplos.astype(jnp.bfloat16)

    def one_block(operands):
        observed_block, start_block, end_block = operands
        _, forward_store = forward_pass(start_block, haplos, observed_block, rates)
        _, backward_store = backward_pass(end_block, haplos, observed_block, rates)
        forward_store = lax.optimization_barrier(forward_store)
        backward_store = lax.optimization_barrier(backward_store)
        carrying = backward_store * allele_half[:, None, :]
        forward_wide = forward_store.astype(jnp.float32)
        numer = jnp.einsum("mtk,mtk->mt", forward_wide, carrying.astype(jnp.float32))
        denom = jnp.einsum("mtk,mtk->mt", forward_wide, backward_store.astype(jnp.float32))
        return numer / denom

    dosage = lax.map(one_block, (observed_blocks, start_blocks, end_blocks))
    return dosage.transpose(1, 0, 2).reshape(MARKERS, TARGETS)
```

```python
import functools

import jax
import jax.numpy as jnp
from jax import lax
from jax.experimental import pallas as pl
from jax.experimental.pallas import tpu as pltpu
from jax.sharding import Mesh, PartitionSpec as P

K = 15360
MARKERS = 240
GROUPS = 16
SPAN = 15
TILES = 15
TGT = 4
BLOCKS = MARKERS // 3
LANES = 128
MSG = 384
hit = 0.99
miss = 0.01
map_unit = 100000.0
lift = float(2**60)


def full(value):
    return jnp.broadcast_to(value, (8, LANES))


def total(tile):
    rows = jnp.sum(tile, axis=0, keepdims=True)
    return full(jnp.sum(rows, axis=1, keepdims=True))


def swapped_blocks(tiles, lane):
    tiles = list(tiles)
    for step in (1, 2, 4):
        low = (lane & (16 * step)) == 0
        for j in range(8):
            if j & step:
                continue
            first, second = tiles[j], tiles[j + step]
            tiles[j] = jnp.where(low, first, pltpu.roll(second, 16 * step, 1))
            tiles[j + step] = jnp.where(low, pltpu.roll(first, LANES - 16 * step, 1), second)
    return tiles


def kernel(place, beta, keep, em, own, other, weights_start, weights_end, emv, out,
           words, fwd, bwd, fstore, bstore, counts_in, sums, gv, gs, nd, sem):
    group = place[0]
    core = lax.rem(group, 2)
    lane = lax.broadcasted_iota(jnp.int32, (8, LANES), 1)
    upper = lax.broadcasted_iota(jnp.int32, (8, LANES), 0) < 4

    def unpack(z, carry):
        for ref, which in ((own, core), (other, 1 - core)):
            tiles = []
            for j in range(8):
                parts = [ref[pl.ds(j * 24 + z * 3 + a, 4, stride=192), :] for a in range(2)]
                tiles.append(jnp.concatenate(parts, axis=0))
            tiles = swapped_blocks(tiles, lane)
            first = (2 * z + which) * SPAN
            for m in range(SPAN):
                tile = tiles[m % 8]
                turned = pltpu.roll(tile, 4, 0)
                low, high = (tile, turned) if m < 8 else (turned, tile)
                words[first + m] = jnp.where(upper, low, lax.shift_right_logical(high, 15))
        return carry

    lax.fori_loop(0, 8, unpack, 0)

    def count(block, carry):
        w0, w1, w2 = [words[3 * block + j] & 0x7FFF for j in range(3)]
        w01, w12, w02 = w0 & w1, w1 & w2, w0 & w2
        for q, w in enumerate((w0, w1, w2, w01, w12, w02, w01 & w2)):
            ones = lax.population_count(w).astype(jnp.float32)
            counts_in[q, pl.ds(block, 1), :] = jnp.sum(ones, axis=0, keepdims=True)
        return carry

    lax.fori_loop(0, BLOCKS, count, 0)
    ones = jnp.ones((8, LANES), jnp.bfloat16)
    n = []
    for q in range(7):
        table = counts_in[q].astype(jnp.bfloat16)
        n.append(lax.dot_general(ones, table, (((1,), (1,)), ((), ())), preferred_element_type=jnp.float32))
    n0, n1, n2, n01, n12, n02, n012 = n
    a1, a0, b1, b0, c1, c0 = [emv[j] for j in range(6)]

    def pair(x1, x0, y1, y0, nx, ny, nxy):
        return nxy * (x1 * y1) + (nx - nxy) * (x1 * y0) + (ny - nxy) * (x0 * y1) + (K - nx - ny + nxy) * (x0 * y0)

    gv[0:8, :] = n0 * a1 + (K - n0) * a0
    gv[8:16, :] = n1 * b1 + (K - n1) * b0
    gv[16:24, :] = n2 * c1 + (K - n2) * c0
    gv[24:32, :] = pair(a1, a0, b1, b0, n0, n1, n01)
    gv[32:40, :] = pair(b1, b0, c1, c0, n1, n2, n12)
    with_a = n012 * (b1 * c1) + (n01 - n012) * (b1 * c0) + (n02 - n012) * (b0 * c1) + (n0 - n01 - n02 + n012) * (b0 * c0)
    rest = (n12 - n012) * (b1 * c1) + (n1 - n01 - n12 + n012) * (b1 * c0) + (n2 - n02 - n12 + n012) * (b0 * c1) \
        + (K - n0 - n1 - n2 + n01 + n12 + n02 - n012) * (b0 * c0)
    gv[40:48, :] = a1 * with_a + a0 * rest
    copy = pltpu.make_async_copy(gv, gs, sem)
    copy.start()
    copy.wait()

    for t in range(TGT):
        for v in range(TILES):
            fwd[t, v] = weights_start[t, v]
            bwd[t, v] = weights_end[t, v]

    def sum_of(ref):
        sums_now = []
        for t in range(TGT):
            acc = ref[t, 0]
            for v in range(1, TILES):
                acc = acc + ref[t, v]
            sums_now.append(total(acc))
        return tuple(sums_now)

    def three(state, block, carry, reverse):
        order = (2, 1, 0) if reverse else (0, 1, 2)
        shift = 1 if reverse else 0
        marks = [3 * block + j for j in order]
        tile_words = [words[m] for m in marks]
        rates = [beta[m + shift] for m in marks]
        singles = order
        pairs = (4, 3) if reverse else (3, 4)
        result = [None] * TGT
        new_scale = [jnp.ones((8, LANES), jnp.float32)] * TGT
        for half in range(2):
            pass
        sums_of = {}
        emis = {t: [(em[m * 8 + 2 * t], em[m * 8 + 2 * t + 1]) for m in marks] for t in range(TGT)}

        def down(targets):
            accs = {t: [None] * 3 for t in targets}
            first = {t: (emis[t][0][0] * carry[4 + t], emis[t][0][1] * carry[4 + t]) for t in targets}
            for v in range(TILES):
                masks = [(w & (1 << v)) != 0 for w in tile_words]
                for t in targets:
                    y = state[t, v]
                    for j in range(3):
                        e1, e0 = first[t] if j == 0 else emis[t][j]
                        y = y * jnp.where(masks[j], e1, e0)
                        accs[t][j] = y if v == 0 else accs[t][j] + y
                    state[t, v] = y
            for t in targets:
                sums_of[t] = [total(a) for a in accs[t]]

        def up(targets):
            mix = {}
            for t in targets:
                q1, q2, q3 = sums_of[t]
                g = lambda q: gs[8 * q + t, block]
                m0 = rates[0] * (carry[t] * carry[4 + t])
                s1 = q1 + m0 * g(singles[0])
                m1 = rates[1] * s1
                s2 = (q2 + m0 * g(pairs[0])) + m1 * g(singles[1])
                m2 = rates[2] * s2
                s3 = (q3 + m0 * g(5)) + m1 * g(pairs[1]) + m2 * g(singles[2])
                result[t] = s3
                mix[t] = (m0 * emis[t][0][0] + m1, m0 * emis[t][0][1] + m1, m2)
            for v in range(TILES):
                masks = [(w & (1 << v)) != 0 for w in tile_words]
                for t in targets:
                    h = jnp.where(masks[0], mix[t][0], mix[t][1])
                    h = h * jnp.where(masks[1], *emis[t][1]) + mix[t][2]
                    h = h * jnp.where(masks[2], *emis[t][2])
                    state[t, v] = state[t, v] + h

        down((0, 1))
        down((2, 3))
        up((0, 1))
        up((2, 3))
        return tuple(result) + tuple(new_scale)

    def run(state, first, count_groups, reverse):
        def one_group(i, sums_now):
            block = (first - i if reverse else first + i) * 5
            carry = tuple(sums_now) + tuple(lift / s for s in sums_now)
            def one_block(j, carry):
                return three(state, block + (4 - j if reverse else j), carry, reverse)
            return lax.fori_loop(0, 5, one_block, carry)[:TGT]
        return lax.fori_loop(0, count_groups, one_group, sum_of(state))

    fsum = run(fwd, 0, group, False)
    bsum = run(bwd, GROUPS - 1, GROUPS - 1 - group, True)

    begin = group * SPAN
    scale_f = tuple(lift / s for s in fsum)
    scale_b = tuple(lift / s for s in bsum)

    def own_step(i, carry):
        fs, bs, ff, bf = carry[0:4], carry[4:8], carry[8:12], carry[12:16]
        mf, mb = begin + i, begin + SPAN - 1 - i
        wf, wb = words[mf], words[mb]
        fnew, bnew = [], []
        for t in range(TGT):
            mix = beta[mf] * fs[t]
            e1, e0 = em[mf * 8 + 2 * t] * ff[t], em[mf * 8 + 2 * t + 1] * ff[t]
            acc = None
            for v in range(TILES):
                x = (fwd[t, v] + mix) * jnp.where((wf & (1 << v)) != 0, e1, e0)
                fwd[t, v] = x
                fstore[i * TGT + t, v] = x
                acc = x if v == 0 else acc + x
            fnew.append(acc)
        for t in range(TGT):
            mix = beta[mb + 1] * bs[t]
            e1, e0 = em[mb * 8 + 2 * t] * bf[t], em[mb * 8 + 2 * t + 1] * bf[t]
            sums[1, (SPAN - 1 - i) * TGT + t] = bs[t]
            acc = None
            for v in range(TILES):
                b = bwd[t, v] + mix
                bstore[(SPAN - 1 - i) * TGT + t, v] = b
                x = b * jnp.where((wb & (1 << v)) != 0, e1, e0)
                bwd[t, v] = x
                acc = x if v == 0 else acc + x
            bnew.append(acc)
        fnew = [total(a) for a in fnew]
        bnew = [total(a) for a in bnew]
        for t in range(TGT):
            sums[0, i * TGT + t] = fnew[t]
        one = jnp.ones((8, LANES), jnp.float32)
        return tuple(fnew) + tuple(bnew) + (one,) * 8

    lax.fori_loop(0, SPAN, own_step, tuple(fsum) + tuple(bsum) + scale_f + scale_b)

    def dose(i, carry):
        m = begin + i
        w = words[m]
        for t in range(TGT):
            row = i * TGT + t
            by_f = 1.0 / sums[0, row]
            by_b = keep[m + 1] / sums[1, row]
            num = den = None
            for v in range(TILES):
                f = (fstore[row, v] * by_f).astype(jnp.bfloat16).astype(jnp.float32)
                b = (bstore[row, v] * by_b).astype(jnp.bfloat16).astype(jnp.float32)
                p = f * b
                q = jnp.where((w & (1 << v)) != 0, p, 0.0)
                num = q if v == 0 else num + q
                den = p if v == 0 else den + p
            nd[0, t, pl.ds(i, 1), :] = jnp.sum(num, axis=0, keepdims=True)
            nd[1, t, pl.ds(i, 1), :] = jnp.sum(den, axis=0, keepdims=True)
        return carry

    lax.fori_loop(0, SPAN, dose, 0)
    column = lax.broadcasted_iota(jnp.int32, (SPAN, LANES), 1)
    answer = jnp.zeros((SPAN, LANES), jnp.float32)
    for t in range(TGT):
        num = jnp.sum(nd[0, t, 0:SPAN, :], axis=1, keepdims=True)
        den = jnp.sum(nd[1, t, 0:SPAN, :], axis=1, keepdims=True)
        answer = jnp.where(column == t, num / den, answer)
    out[...] = answer[:, 0:TGT]


def chains(place, beta, keep, em, own, other, weights_start, weights_end, emv):
    smem = pl.BlockSpec(memory_space=pltpu.SMEM)
    vmem = pl.BlockSpec(memory_space=pltpu.VMEM)
    f32 = jnp.float32
    return pl.pallas_call(
        kernel,
        out_shape=jax.ShapeDtypeStruct((SPAN, TGT), f32),
        in_specs=[smem] * 4 + [vmem] * 5,
        out_specs=vmem,
        scratch_shapes=[
            pltpu.VMEM((MARKERS, 8, LANES), jnp.int32),
            pltpu.VMEM((TGT, TILES, 8, LANES), f32),
            pltpu.VMEM((TGT, TILES, 8, LANES), f32),
            pltpu.VMEM((SPAN * TGT, TILES, 8, LANES), f32),
            pltpu.VMEM((SPAN * TGT, TILES, 8, LANES), f32),
            pltpu.VMEM((7, LANES, LANES), f32),
            pltpu.VMEM((2, SPAN * TGT, 8, LANES), f32),
            pltpu.VMEM((48, LANES), f32),
            pltpu.SMEM((48, LANES), f32),
            pltpu.VMEM((2, TGT, 16, LANES), f32),
            pltpu.SemaphoreType.DMA,
        ],
        compiler_params=pltpu.CompilerParams(vmem_limit_bytes=48 << 20),
    )(place, beta, keep, em, own, other, weights_start, weights_end, emv)


def to_all(array, axes):
    peers = 1
    for axis in axes:
        peers *= lax.axis_size(axis)
    return lax.all_to_all(jnp.broadcast_to(array[None], (peers, *array.shape)), axes, 0, 0, tiled=True)


def planes(weights):
    split = weights.reshape(TGT, 4, LANES, 2, 15)
    return split.transpose(0, 4, 3, 1, 2).reshape(TGT, TILES, 8, LANES)


def local(alleles, observed, map_steps, start_weights, end_weights):
    zero = jnp.zeros
    message = jnp.concatenate([
        alleles.reshape(1, 240), map_steps.reshape(1, 15), zero((1, 1), jnp.int32),
        observed.reshape(1, 60), zero((1, 68), jnp.int32)], axis=1)
    line = to_all(message, ("z",))
    spread = to_all(line.reshape(1, 8 * MSG), ("x", "y"))
    own = spread.reshape(768, LANES)
    other = lax.ppermute(own, "c", [(0, 1), (1, 0)])

    core = lax.axis_index("c")
    small = line[:, 0, 240:316]
    partner = lax.ppermute(small, "c", [(0, 1), (1, 0)])
    both = jnp.stack([jnp.where(core == 0, small, partner), jnp.where(core == 0, partner, small)], axis=1)
    steps = both[:, :, 0:15].reshape(MARKERS)
    seen = both[:, :, 16:76].reshape(MARKERS, TGT)
    rates = 1.0 - jnp.exp(-steps.astype(jnp.float32) / map_unit)
    beta = jnp.concatenate([(rates / K) / (1.0 - rates), zero((16,), jnp.float32)])
    keep = jnp.concatenate([1.0 - rates, jnp.ones((16,), jnp.float32)])
    if_one = jnp.where(seen == 2, 1.0, jnp.where(seen == 1, hit, miss)).astype(jnp.float32)
    if_zero = jnp.where(seen == 2, 1.0, jnp.where(seen == 0, hit, miss)).astype(jnp.float32)
    em = jnp.stack([if_one, if_zero], axis=2)
    emv = em.reshape(BLOCKS, 3, TGT, 2).transpose(1, 3, 2, 0).reshape(6, TGT, BLOCKS)
    emv = jnp.pad(emv, ((0, 0), (0, 8 - TGT), (0, LANES - BLOCKS)))
    place = (2 * lax.axis_index("z") + core).astype(jnp.int32).reshape(1)
    return chains(place, beta, keep, em.reshape(MARKERS * 8), own, other,
                  planes(start_weights), planes(end_weights), emv)


def solution(mesh):
    cut = Mesh(mesh.devices.reshape(8, 2, 4, 8), ("z", "c", "x", "y"))
    grp, hap = ("z", "c"), ("x", "y")
    in_specs = (P(grp, hap), P(grp, hap), P(grp), P(hap, None), P(hap, None))
    return jax.shard_map(local, mesh=cut, in_specs=in_specs, out_specs=P(grp, hap), check_vma=False)
```

```python
import jax
import jax.numpy as jnp
from jax import lax
from jax.experimental import pallas as pl
from jax.experimental.pallas import tpu as pltpu
from jax.sharding import Mesh, PartitionSpec as P

K = 15360
MARKERS = 240
GROUPS = 16
SPAN = 15
TILES = 15
TGT = 4
BLOCKS = MARKERS // 3
LANES = 128
CHUNK = 1920
hit = 0.99
miss = 0.01
map_unit = 100000.0
lift = float(2**60)


def full(value):
    return jnp.broadcast_to(value, (8, LANES))


def total(tile):
    rows = jnp.sum(tile, axis=0, keepdims=True)
    return full(jnp.sum(rows, axis=1, keepdims=True))


def swapped_blocks(tiles, lane):
    tiles = list(tiles)
    for step in (1, 2, 4):
        low = (lane & (16 * step)) == 0
        for j in range(8):
            if j & step:
                continue
            first, second = tiles[j], tiles[j + step]
            tiles[j] = jnp.where(low, first, pltpu.roll(second, 16 * step, 1))
            tiles[j + step] = jnp.where(low, pltpu.roll(first, LANES - 16 * step, 1), second)
    return tiles


def pack_kernel(alleles, observed, steps, message):
    rows = [alleles[m:m + 1, :] for m in range(SPAN)]
    zero = lambda n: jnp.zeros((1, n), jnp.int32)
    first = jnp.concatenate(rows[:8], axis=1)
    second = jnp.concatenate(rows[8:] + [zero(16)], axis=1)
    seen = [observed[t:t + 1, :] for t in range(TGT)]
    third = jnp.concatenate([steps[...], zero(1)] + seen + [zero(52)], axis=1)
    message[...] = jnp.concatenate([first, second, third] * 8, axis=0)


def pack(alleles, observed, steps):
    vmem = pl.BlockSpec(memory_space=pltpu.VMEM)
    return pl.pallas_call(
        pack_kernel, out_shape=jax.ShapeDtypeStruct((24, LANES), jnp.int32),
        in_specs=[vmem] * 3, out_specs=vmem)(alleles, observed, steps)


def planes_kernel(weights_start, weights_end, start, end, stage, tiles):
    lane = lax.broadcasted_iota(jnp.int32, (8, LANES), 1)
    pair_of = []
    for u in range(TILES):
        offset = (LANES * u) % 30 + lane
        pair_of.append(lax.shift_right_logical(offset - 30 * lax.shift_right_logical(offset * 2185, 16), 1))
    for which, weights in enumerate((weights_start, weights_end)):
        for u in range(TILES):
            for s in range(8):
                at = CHUNK * s + LANES * u
                stage[u, 4 * s:4 * s + 4, :] = weights[:, at:at + LANES]
            for t in range(TGT):
                tiles[which * TGT + t, u] = stage[u, pl.ds(t, 8, stride=4), :]
    for p in range(TILES):
        masks = [pair_of[u] == p for u in range(1, TILES)]
        for row in range(2 * TGT):
            chosen = tiles[row, 0]
            for u in range(1, TILES):
                chosen = jnp.where(masks[u - 1], tiles[row, u], chosen)
            if p:
                chosen = pltpu.roll(chosen, LANES - 2 * p, 1)
            if row < TGT:
                start[row, p] = chosen
            else:
                end[row - TGT, p] = chosen


def planes(weights_start, weights_end):
    vmem = pl.BlockSpec(memory_space=pltpu.VMEM)
    laid = jax.ShapeDtypeStruct((TGT, TILES, 8, LANES), jnp.float32)
    return pl.pallas_call(
        planes_kernel,
        out_shape=(laid, laid),
        in_specs=[vmem] * 2, out_specs=(vmem,) * 2,
        scratch_shapes=[pltpu.VMEM((TILES, 32, LANES), jnp.float32), pltpu.VMEM((2 * TGT, TILES, 8, LANES), jnp.float32)],
        cost_estimate=pl.CostEstimate(flops=4_000_000, transcendentals=0, bytes_accessed=1_000_000),
    )(weights_start, weights_end)


def home_of(group):
    return lax.shift_right_logical(group, 1) + 8 * (group & 1)


def emissions_by_block(sides):
    found = []
    values = sides.astype(jnp.float32).astype(jnp.bfloat16)
    block = lax.broadcasted_iota(jnp.int32, (1, LANES), 1)
    group = lax.shift_right_logical(block * 13108, 16)
    within = block - 5 * group
    home = lax.shift_right_logical(group, 1) + 8 * (group & 1)
    mine = lax.broadcasted_iota(jnp.int32, (16, LANES), 0) == home
    source = lax.broadcasted_iota(jnp.int32, (LANES, LANES), 0)
    for q in range(3):
        rows = []
        for t in range(TGT):
            pick = (source == 16 + 15 * t + 3 * within + q).astype(jnp.float32).astype(jnp.bfloat16)
            moved = jnp.dot(values, pick, preferred_element_type=jnp.float32)
            rows.append(jnp.sum(jnp.where(mine, moved, 0.0), axis=0, keepdims=True))
        seen = jnp.concatenate(rows + rows, axis=0)
        found.append(jnp.where(seen == 2.0, 1.0, jnp.where(seen == 1.0, hit, miss)))
        found.append(jnp.where(seen == 2.0, 1.0, jnp.where(seen == 0.0, hit, miss)))
    return found


def kernel(place, beta, keep, for_one, for_zero, sides, own, other, weights_start, weights_end, out,
           words, fwd, bwd, fstore, bstore, counts_in, sums, gv, gs, nd, eb, sem, weight_sems):
    loads = [pltpu.make_async_copy(weights_start, fwd, weight_sems.at[0]),
             pltpu.make_async_copy(weights_end, bwd, weight_sems.at[1])]
    for load in loads:
        load.start()
    group = place[0]
    core = lax.rem(group, 2)
    lane = lax.broadcasted_iota(jnp.int32, (8, LANES), 1)
    half_lane = lax.shift_right_logical(lane, 1)
    odd = lane & 1
    word_at = (47 * half_lane) & 63

    def unpack(z, carry):
        for ref, which in ((own, core), (other, 1 - core)):
            tiles = [ref[pl.ds(16 * q + 2 * z + a, 8, stride=64), :] for a in range(2) for q in range(4)]
            tiles = swapped_blocks(tiles, lane)
            first = (2 * z + which) * SPAN
            for m in range(SPAN):
                picked = jnp.take_along_axis(tiles[m % 8], word_at + (64 if m >= 8 else 0), axis=1)
                words[first + m] = lax.shift_right_logical(picked, odd)
        return carry

    lax.fori_loop(0, 8, unpack, 0, unroll=4)

    def emission(row, m, t):
        at = 16 + 15 * t + m
        return for_one[row, at], for_zero[row, at]

    def count(block, carry):
        w0, w1, w2 = [words[3 * block + j] & 0x15555555 for j in range(3)]
        w01, w12, w02 = w0 & w1, w1 & w2, w0 & w2
        for q, w in enumerate((w0, w1, w2, w01, w12, w02, w01 & w2)):
            ones = lax.population_count(w).astype(jnp.float32)
            counts_in[q, pl.ds(block, 1), :] = jnp.sum(ones, axis=0, keepdims=True)
        return carry

    lax.fori_loop(0, BLOCKS, count, 0, unroll=4)
    ones = jnp.ones((8, LANES), jnp.bfloat16)
    n = []
    for q in range(7):
        table = counts_in[q].astype(jnp.bfloat16)
        n.append(lax.dot_general(ones, table, (((1,), (1,)), ((), ())), preferred_element_type=jnp.float32))
    n0, n1, n2, n01, n12, n02, n012 = n
    a1, a0, b1, b0, c1, c0 = emissions_by_block(sides[...])

    def pair(x1, x0, y1, y0, nx, ny, nxy):
        return nxy * (x1 * y1) + (nx - nxy) * (x1 * y0) + (ny - nxy) * (x0 * y1) + (K - nx - ny + nxy) * (x0 * y0)

    table0 = n0 * a1 + (K - n0) * a0
    table1 = n1 * b1 + (K - n1) * b0
    table2 = n2 * c1 + (K - n2) * c0
    table3 = pair(a1, a0, b1, b0, n0, n1, n01)
    table4 = pair(b1, b0, c1, c0, n1, n2, n12)
    with_a = n012 * (b1 * c1) + (n01 - n012) * (b1 * c0) + (n02 - n012) * (b0 * c1) + (n0 - n01 - n02 + n012) * (b0 * c0)
    rest = (n12 - n012) * (b1 * c1) + (n1 - n01 - n12 + n012) * (b1 * c0) + (n2 - n02 - n12 + n012) * (b0 * c1) \
        + (K - n0 - n1 - n2 + n01 + n12 + n02 - n012) * (b0 * c0)
    table5 = a1 * with_a + a0 * rest
    for i, table in enumerate((table0, table1, table2, table3, table4, table5)):
        gv[TGT * i:TGT * i + TGT, :] = table[0:TGT]
    copy = pltpu.make_async_copy(gv, gs, sem)
    copy.start()

    for load in loads:
        load.wait()

    def sum_of(ref):
        sums_now = []
        for t in range(TGT):
            acc = ref[t, 0]
            for v in range(1, TILES):
                acc = acc + ref[t, v]
            sums_now.append(total(acc))
        return tuple(sums_now)

    def three(state, block, carry, reverse):
        order = (2, 1, 0) if reverse else (0, 1, 2)
        step = block - 5 * lax.shift_right_logical(block * 13108, 16)
        at = lax.shift_right_logical(block * 13108, 16)
        row = home_of(at)
        tile_words = [words[3 * block + j] for j in order]
        if reverse:
            last = step == 4
            after = jnp.where(last, home_of(jnp.minimum(at + 1, GROUPS - 1)), row)
            edge = beta[after, jnp.where(last, 0, 3 * step + 3)]
            edge = jnp.where(block == BLOCKS - 1, 0.0, edge)
            rates = [edge, beta[row, 3 * step + 2], beta[row, 3 * step + 1]]
        else:
            rates = [beta[row, 3 * step + j] for j in range(3)]
        singles = order
        pairs = (4, 3) if reverse else (3, 4)
        result = [None] * TGT
        new_scale = [jnp.ones((8, LANES), jnp.float32)] * TGT
        sums_of = {}
        emis = {t: [emission(row, 3 * step + j, t) for j in order] for t in range(TGT)}

        def down(targets):
            accs = {t: [None] * 3 for t in targets}
            first = {t: (emis[t][0][0] * carry[4 + t], emis[t][0][1] * carry[4 + t]) for t in targets}
            for v in range(TILES):
                masks = [(w & (1 << (2 * v))) != 0 for w in tile_words]
                for t in targets:
                    y = state[t, v]
                    for j in range(3):
                        e1, e0 = first[t] if j == 0 else emis[t][j]
                        e = jnp.where(masks[j], e1, e0)
                        if j:
                            eb[j - 1, t, v] = e
                        y = y * e
                        accs[t][j] = y if v == 0 else accs[t][j] + y
                    state[t, v] = y
            for t in targets:
                sums_of[t] = [total(a) for a in accs[t]]

        def up(targets):
            mix = {}
            for t in targets:
                q1, q2, q3 = sums_of[t]
                g = lambda q: gs[TGT * q + t, block]
                m0 = rates[0] * (carry[t] * carry[4 + t])
                s1 = q1 + m0 * g(singles[0])
                m1 = rates[1] * s1
                s2 = (q2 + m0 * g(pairs[0])) + m1 * g(singles[1])
                m2 = rates[2] * s2
                s3 = (q3 + m0 * g(5)) + m1 * g(pairs[1]) + m2 * g(singles[2])
                result[t] = s3
                mix[t] = (m0 * emis[t][0][0] + m1, m0 * emis[t][0][1] + m1, m2)
            for v in range(TILES):
                mask = (tile_words[0] & (1 << (2 * v))) != 0
                for t in targets:
                    h = jnp.where(mask, mix[t][0], mix[t][1])
                    h = h * eb[0, t, v] + mix[t][2]
                    h = h * eb[1, t, v]
                    state[t, v] = state[t, v] + h

        down((0, 1))
        down((2, 3))
        up((0, 1))
        up((2, 3))
        return tuple(result) + tuple(new_scale)

    start_sums, end_sums = sum_of(fwd), sum_of(bwd)
    copy.wait()

    def run(state, first, count_groups, reverse, sums_now):
        def one_group(i, sums_now):
            block = (first - i if reverse else first + i) * 5
            carry = tuple(sums_now) + tuple(lift / s for s in sums_now)
            def one_block(j, carry):
                return three(state, block + (4 - j if reverse else j), carry, reverse)
            return lax.fori_loop(0, 5, one_block, carry, unroll=5)[:TGT]
        return lax.fori_loop(0, count_groups, one_group, sums_now)

    fsum = run(fwd, 0, group, False, start_sums)
    bsum = run(bwd, GROUPS - 1, GROUPS - 1 - group, True, end_sums)

    begin = group * SPAN
    here = home_of(group)
    after = home_of(jnp.minimum(group + 1, GROUPS - 1))

    def later(m):
        last = m == SPAN - 1
        return jnp.where(last, after, here), jnp.where(last, 0, m + 1), jnp.logical_and(last, group == GROUPS - 1)

    scale_f = tuple(lift / s for s in fsum)
    scale_b = tuple(lift / s for s in bsum)

    def own_step(i, carry):
        fs, bs, ff, bf = carry[0:4], carry[4:8], carry[8:12], carry[12:16]
        up_to = SPAN - 1 - i
        wf, wb = words[begin + i], words[begin + up_to]
        row, at, none = later(up_to)
        rate_b = jnp.where(none, 0.0, beta[row, at])
        fnew, bnew = [], []
        for t in range(TGT):
            mix = beta[here, i] * fs[t]
            e1, e0 = emission(here, i, t)
            e1, e0 = e1 * ff[t], e0 * ff[t]
            acc = None
            for v in range(TILES):
                x = (fwd[t, v] + mix) * jnp.where((wf & (1 << (2 * v))) != 0, e1, e0)
                fwd[t, v] = x
                fstore[i * TGT + t, v] = x
                acc = x if v == 0 else acc + x
            fnew.append(acc)
        for t in range(TGT):
            mix = rate_b * bs[t]
            e1, e0 = emission(here, up_to, t)
            e1, e0 = e1 * bf[t], e0 * bf[t]
            sums[1, (SPAN - 1 - i) * TGT + t] = bs[t]
            acc = None
            for v in range(TILES):
                b = bwd[t, v] + mix
                bstore[(SPAN - 1 - i) * TGT + t, v] = b
                x = b * jnp.where((wb & (1 << (2 * v))) != 0, e1, e0)
                bwd[t, v] = x
                acc = x if v == 0 else acc + x
            bnew.append(acc)
        fnew = [total(a) for a in fnew]
        bnew = [total(a) for a in bnew]
        for t in range(TGT):
            sums[0, i * TGT + t] = fnew[t]
        one = jnp.ones((8, LANES), jnp.float32)
        return tuple(fnew) + tuple(bnew) + (one,) * 8

    lax.fori_loop(0, SPAN, own_step, tuple(fsum) + tuple(bsum) + scale_f + scale_b, unroll=3)

    def dose(i, carry):
        w = words[begin + i]
        at_row, at, none = later(i)
        kept = jnp.where(none, 1.0, keep[at_row, at])
        for t in range(TGT):
            row = i * TGT + t
            by_f = 1.0 / sums[0, row]
            by_b = kept / sums[1, row]
            num = den = None
            for v in range(TILES):
                f = (fstore[row, v] * by_f).astype(jnp.bfloat16).astype(jnp.float32)
                b = (bstore[row, v] * by_b).astype(jnp.bfloat16).astype(jnp.float32)
                p = f * b
                q = jnp.where((w & (1 << (2 * v))) != 0, p, 0.0)
                num = q if v == 0 else num + q
                den = p if v == 0 else den + p
            nd[0, t, pl.ds(i, 1), :] = jnp.sum(num, axis=0, keepdims=True)
            nd[1, t, pl.ds(i, 1), :] = jnp.sum(den, axis=0, keepdims=True)
        return carry

    lax.fori_loop(0, SPAN, dose, 0, unroll=3)
    line = jnp.ones((8, LANES), jnp.float32)
    which = lax.broadcasted_iota(jnp.int32, (8, 16), 0)
    answer = jnp.zeros((8, 16), jnp.float32)
    for t in range(TGT):
        num, den = [
            lax.dot_general(line, nd[i, t], (((1,), (1,)), ((), ())), precision=lax.Precision.HIGHEST,
                            preferred_element_type=jnp.float32) for i in range(2)]
        answer = jnp.where(which == t, num / den, answer)
    out[...] = answer[0:TGT, 0:SPAN]


def chains(place, beta, keep, for_one, for_zero, sides, own, other, weights_start, weights_end):
    smem = pl.BlockSpec(memory_space=pltpu.SMEM)
    vmem = pl.BlockSpec(memory_space=pltpu.VMEM)
    f32 = jnp.float32
    return pl.pallas_call(
        kernel,
        out_shape=jax.ShapeDtypeStruct((TGT, SPAN), f32),
        in_specs=[smem] * 5 + [vmem] * 3 + [pl.BlockSpec(memory_space=pl.ANY)] * 2,
        out_specs=vmem,
        scratch_shapes=[
            pltpu.VMEM((MARKERS, 8, LANES), jnp.int32),
            pltpu.VMEM((TGT, TILES, 8, LANES), f32),
            pltpu.VMEM((TGT, TILES, 8, LANES), f32),
            pltpu.VMEM((SPAN * TGT, TILES, 8, LANES), f32),
            pltpu.VMEM((SPAN * TGT, TILES, 8, LANES), f32),
            pltpu.VMEM((7, LANES, LANES), f32),
            pltpu.VMEM((2, SPAN * TGT, 8, LANES), f32),
            pltpu.VMEM((24, LANES), f32),
            pltpu.SMEM((24, LANES), f32),
            pltpu.VMEM((2, TGT, 16, LANES), f32),
            pltpu.VMEM((2, TGT, TILES, 8, LANES), f32),
            pltpu.SemaphoreType.DMA,
            pltpu.SemaphoreType.DMA((2,)),
        ],
        compiler_params=pltpu.CompilerParams(vmem_limit_bytes=60 << 20),
    )(place, beta, keep, for_one, for_zero, sides, own, other, weights_start, weights_end)


def local(alleles, observed, map_steps, start_weights, end_weights):
    message = pack(alleles, observed.T, map_steps.reshape(1, SPAN)).reshape(8, 1, 384)
    start, end = planes(start_weights, end_weights)
    line = lax.all_to_all(message, "z", 0, 0, tiled=True)
    spread = jnp.broadcast_to(line[:, :, 0:256].reshape(1, 1, 2048), (32, 1, 2048))
    own = lax.all_to_all(spread, ("x", "y"), 0, 0, tiled=True).reshape(512, LANES)
    side = line[:, 0, 256:384]
    swap = [(0, 1), (1, 0)]
    other = lax.ppermute(own, "c", swap)
    partner = lax.ppermute(side, "c", swap)

    core = lax.axis_index("c")
    sides = jnp.concatenate([jnp.where(core == 0, side, partner), jnp.where(core == 0, partner, side)], axis=0)
    rates = 1.0 - jnp.exp(-sides.astype(jnp.float32) / map_unit)
    keep = 1.0 - rates
    beta = (rates / K) / keep
    for_one = jnp.where(sides == 2, 1.0, jnp.where(sides == 1, hit, miss)).astype(jnp.float32)
    for_zero = jnp.where(sides == 2, 1.0, jnp.where(sides == 0, hit, miss)).astype(jnp.float32)
    place = (2 * lax.axis_index("z") + core).astype(jnp.int32).reshape(1)
    return chains(place, beta, keep, for_one, for_zero, sides, own, other, start, end).T


def solution(mesh):
    cut = Mesh(mesh.devices.reshape(8, 2, 4, 8), ("z", "c", "x", "y"))
    grp, hap = ("z", "c"), ("x", "y")
    in_specs = (P(grp, hap), P(grp, hap), P(grp), P(hap, None), P(hap, None))
    return jax.shard_map(local, mesh=cut, in_specs=in_specs, out_specs=P(grp, hap), check_vma=False)
```

```python
import jax
import jax.numpy as jnp
from jax import lax
from jax.experimental import pallas as pl
from jax.experimental.pallas import tpu as pltpu
from jax.sharding import Mesh, PartitionSpec as P

K = 15360
MARKERS = 240
GROUPS = 16
SPAN = 15
TILES = 15
TGT = 4
BLOCKS = MARKERS // 3
LANES = 128
CHUNK = 1920
hit = 0.99
miss = 0.01
map_unit = 100000.0
lift = float(2**60)


def full(value):
    return jnp.broadcast_to(value, (8, LANES))


def total(tile):
    rows = jnp.sum(tile, axis=0, keepdims=True)
    return full(jnp.sum(rows, axis=1, keepdims=True))


def swapped_blocks(tiles, lane):
    tiles = list(tiles)
    for step in (1, 2, 4):
        low = (lane & (16 * step)) == 0
        for j in range(8):
            if j & step:
                continue
            first, second = tiles[j], tiles[j + step]
            tiles[j] = jnp.where(low, first, pltpu.roll(second, 16 * step, 1))
            tiles[j + step] = jnp.where(low, pltpu.roll(first, LANES - 16 * step, 1), second)
    return tiles


def pack_kernel(alleles, observed, steps, message):
    rows = [alleles[m:m + 1, :] for m in range(SPAN)]
    zero = lambda n: jnp.zeros((1, n), jnp.int32)
    first = jnp.concatenate(rows[:8], axis=1)
    second = jnp.concatenate(rows[8:] + [zero(16)], axis=1)
    seen = [observed[t:t + 1, :] for t in range(TGT)]
    third = jnp.concatenate([steps[...], zero(1)] + seen + [zero(52)], axis=1)
    message[...] = jnp.concatenate([first, second, third] * 8, axis=0)


def pack(alleles, observed, steps):
    vmem = pl.BlockSpec(memory_space=pltpu.VMEM)
    return pl.pallas_call(
        pack_kernel, out_shape=jax.ShapeDtypeStruct((24, LANES), jnp.int32),
        in_specs=[vmem] * 3, out_specs=vmem)(alleles, observed, steps)


def planes_kernel(weights_start, weights_end, start, end, stage, tiles):
    lane = lax.broadcasted_iota(jnp.int32, (8, LANES), 1)
    pair_of = []
    for u in range(TILES):
        offset = (LANES * u) % 30 + lane
        pair_of.append(lax.shift_right_logical(offset - 30 * lax.shift_right_logical(offset * 2185, 16), 1))
    for which, weights in enumerate((weights_start, weights_end)):
        for u in range(TILES):
            for s in range(8):
                at = CHUNK * s + LANES * u
                stage[u, 4 * s:4 * s + 4, :] = weights[:, at:at + LANES]
            for t in range(TGT):
                tiles[which * TGT + t, u] = stage[u, pl.ds(t, 8, stride=4), :]
    for p in range(TILES):
        masks = [pair_of[u] == p for u in range(1, TILES)]
        for row in range(2 * TGT):
            chosen = tiles[row, 0]
            for u in range(1, TILES):
                chosen = jnp.where(masks[u - 1], tiles[row, u], chosen)
            if p:
                chosen = pltpu.roll(chosen, LANES - 2 * p, 1)
            if row < TGT:
                start[row, p] = chosen
            else:
                end[row - TGT, p] = chosen


def planes(weights_start, weights_end):
    vmem = pl.BlockSpec(memory_space=pltpu.VMEM)
    laid = jax.ShapeDtypeStruct((TGT, TILES, 8, LANES), jnp.float32)
    return pl.pallas_call(
        planes_kernel,
        out_shape=(laid, laid),
        in_specs=[vmem] * 2, out_specs=(vmem,) * 2,
        scratch_shapes=[pltpu.VMEM((TILES, 32, LANES), jnp.float32), pltpu.VMEM((2 * TGT, TILES, 8, LANES), jnp.float32)],
        cost_estimate=pl.CostEstimate(flops=4_000_000, transcendentals=0, bytes_accessed=1_000_000),
    )(weights_start, weights_end)


def home_of(group):
    return lax.shift_right_logical(group, 1) + 8 * (group & 1)


def emissions_by_block(sides):
    found = []
    values = sides.astype(jnp.float32).astype(jnp.bfloat16)
    block = lax.broadcasted_iota(jnp.int32, (1, LANES), 1)
    group = lax.shift_right_logical(block * 13108, 16)
    within = block - 5 * group
    home = lax.shift_right_logical(group, 1) + 8 * (group & 1)
    mine = lax.broadcasted_iota(jnp.int32, (16, LANES), 0) == home
    source = lax.broadcasted_iota(jnp.int32, (LANES, LANES), 0)
    for q in range(3):
        rows = []
        for t in range(TGT):
            pick = (source == 16 + 15 * t + 3 * within + q).astype(jnp.float32).astype(jnp.bfloat16)
            moved = jnp.dot(values, pick, preferred_element_type=jnp.float32)
            rows.append(jnp.sum(jnp.where(mine, moved, 0.0), axis=0, keepdims=True))
        seen = jnp.concatenate(rows + rows, axis=0)
        found.append(jnp.where(seen == 2.0, 1.0, jnp.where(seen == 1.0, hit, miss)))
        found.append(jnp.where(seen == 2.0, 1.0, jnp.where(seen == 0.0, hit, miss)))
    return found


def kernel(place, beta, keep, for_one, for_zero, sides, own, other, weights_start, weights_end, out,
           words, fwd, bwd, fstore, bstore, counts_in, sums, gv, gs, nd, eb, sem, weight_sems):
    loads = [pltpu.make_async_copy(weights_start, fwd, weight_sems.at[0]),
             pltpu.make_async_copy(weights_end, bwd, weight_sems.at[1])]
    for load in loads:
        load.start()
    group = place[0]
    core = lax.rem(group, 2)
    lane = lax.broadcasted_iota(jnp.int32, (8, LANES), 1)
    half_lane = lax.shift_right_logical(lane, 1)
    odd = lane & 1
    word_at = (47 * half_lane) & 63

    def unpack(z, carry):
        for ref, which in ((own, core), (other, 1 - core)):
            tiles = [ref[pl.ds(16 * q + 2 * z + a, 8, stride=64), :] for a in range(2) for q in range(4)]
            tiles = swapped_blocks(tiles, lane)
            first = (2 * z + which) * SPAN
            for m in range(SPAN):
                picked = jnp.take_along_axis(tiles[m % 8], word_at + (64 if m >= 8 else 0), axis=1)
                words[first + m] = lax.shift_right_logical(picked, odd)
        return carry

    lax.fori_loop(0, 8, unpack, 0, unroll=2)

    def emission(row, m, t):
        at = 16 + 15 * t + m
        return for_one[row, at], for_zero[row, at]

    def count(block, carry):
        w0, w1, w2 = [words[3 * block + j] & 0x15555555 for j in range(3)]
        w01, w12, w02 = w0 & w1, w1 & w2, w0 & w2
        for q, w in enumerate((w0, w1, w2, w01, w12, w02, w01 & w2)):
            ones = lax.population_count(w).astype(jnp.float32)
            counts_in[q, pl.ds(block, 1), :] = jnp.sum(ones, axis=0, keepdims=True)
        return carry

    lax.fori_loop(0, BLOCKS, count, 0, unroll=4)
    ones = jnp.ones((8, LANES), jnp.bfloat16)
    n = []
    for q in range(7):
        table = counts_in[q].astype(jnp.bfloat16)
        n.append(lax.dot_general(ones, table, (((1,), (1,)), ((), ())), preferred_element_type=jnp.float32))
    n0, n1, n2, n01, n12, n02, n012 = n
    a1, a0, b1, b0, c1, c0 = emissions_by_block(sides[...])

    def pair(x1, x0, y1, y0, nx, ny, nxy):
        return nxy * (x1 * y1) + (nx - nxy) * (x1 * y0) + (ny - nxy) * (x0 * y1) + (K - nx - ny + nxy) * (x0 * y0)

    table0 = n0 * a1 + (K - n0) * a0
    table1 = n1 * b1 + (K - n1) * b0
    table2 = n2 * c1 + (K - n2) * c0
    table3 = pair(a1, a0, b1, b0, n0, n1, n01)
    table4 = pair(b1, b0, c1, c0, n1, n2, n12)
    with_a = n012 * (b1 * c1) + (n01 - n012) * (b1 * c0) + (n02 - n012) * (b0 * c1) + (n0 - n01 - n02 + n012) * (b0 * c0)
    rest = (n12 - n012) * (b1 * c1) + (n1 - n01 - n12 + n012) * (b1 * c0) + (n2 - n02 - n12 + n012) * (b0 * c1) \
        + (K - n0 - n1 - n2 + n01 + n12 + n02 - n012) * (b0 * c0)
    table5 = a1 * with_a + a0 * rest
    for i, table in enumerate((table0, table1, table2, table3, table4, table5)):
        gv[TGT * i:TGT * i + TGT, :] = table[0:TGT]
    copy = pltpu.make_async_copy(gv, gs, sem)
    copy.start()

    for load in loads:
        load.wait()

    def sum_of(ref):
        sums_now = []
        for t in range(TGT):
            acc = ref[t, 0]
            for v in range(1, TILES):
                acc = acc + ref[t, v]
            sums_now.append(total(acc))
        return tuple(sums_now)

    def three(state, block, carry, reverse):
        order = (2, 1, 0) if reverse else (0, 1, 2)
        step = block - 5 * lax.shift_right_logical(block * 13108, 16)
        at = lax.shift_right_logical(block * 13108, 16)
        row = home_of(at)
        tile_words = [words[3 * block + j] for j in order]
        if reverse:
            last = step == 4
            after = jnp.where(last, home_of(jnp.minimum(at + 1, GROUPS - 1)), row)
            edge = beta[after, jnp.where(last, 0, 3 * step + 3)]
            edge = jnp.where(block == BLOCKS - 1, 0.0, edge)
            rates = [edge, beta[row, 3 * step + 2], beta[row, 3 * step + 1]]
        else:
            rates = [beta[row, 3 * step + j] for j in range(3)]
        singles = order
        pairs = (4, 3) if reverse else (3, 4)
        result = [None] * TGT
        new_scale = [jnp.ones((8, LANES), jnp.float32)] * TGT
        sums_of = {}
        emis = {t: [emission(row, 3 * step + j, t) for j in order] for t in range(TGT)}

        def down(targets):
            accs = {t: [None] * 3 for t in targets}
            first = {t: (emis[t][0][0] * carry[4 + t], emis[t][0][1] * carry[4 + t]) for t in targets}
            for v in range(TILES):
                masks = [(w & (1 << (2 * v))) != 0 for w in tile_words]
                for t in targets:
                    y = state[t, v]
                    for j in range(3):
                        e1, e0 = first[t] if j == 0 else emis[t][j]
                        e = jnp.where(masks[j], e1, e0)
                        if j:
                            eb[j - 1, t, v] = e
                        y = y * e
                        accs[t][j] = y if v == 0 else accs[t][j] + y
                    state[t, v] = y
            for t in targets:
                sums_of[t] = [total(a) for a in accs[t]]

        def up(targets):
            mix = {}
            for t in targets:
                q1, q2, q3 = sums_of[t]
                g = lambda q: gs[TGT * q + t, block]
                m0 = rates[0] * (carry[t] * carry[4 + t])
                s1 = q1 + m0 * g(singles[0])
                m1 = rates[1] * s1
                s2 = (q2 + m0 * g(pairs[0])) + m1 * g(singles[1])
                m2 = rates[2] * s2
                s3 = (q3 + m0 * g(5)) + m1 * g(pairs[1]) + m2 * g(singles[2])
                result[t] = s3
                mix[t] = (m0 * emis[t][0][0] + m1, m0 * emis[t][0][1] + m1, m2)
            for v in range(TILES):
                mask = (tile_words[0] & (1 << (2 * v))) != 0
                for t in targets:
                    h = jnp.where(mask, mix[t][0], mix[t][1])
                    h = h * eb[0, t, v] + mix[t][2]
                    h = h * eb[1, t, v]
                    state[t, v] = state[t, v] + h

        down((0, 1))
        down((2, 3))
        up((0, 1))
        up((2, 3))
        return tuple(result) + tuple(new_scale)

    start_sums, end_sums = sum_of(fwd), sum_of(bwd)
    copy.wait()

    def run(state, first, count_groups, reverse, sums_now):
        def one_group(i, sums_now):
            block = (first - i if reverse else first + i) * 5
            carry = tuple(sums_now) + tuple(lift / s for s in sums_now)
            def one_block(j, carry):
                return three(state, block + (4 - j if reverse else j), carry, reverse)
            return lax.fori_loop(0, 5, one_block, carry, unroll=5)[:TGT]
        return lax.fori_loop(0, count_groups, one_group, sums_now)

    fsum = run(fwd, 0, group, False, start_sums)
    bsum = run(bwd, GROUPS - 1, GROUPS - 1 - group, True, end_sums)

    begin = group * SPAN
    here = home_of(group)
    after = home_of(jnp.minimum(group + 1, GROUPS - 1))

    def later(m):
        last = m == SPAN - 1
        return jnp.where(last, after, here), jnp.where(last, 0, m + 1), jnp.logical_and(last, group == GROUPS - 1)

    scale_f = tuple(lift / s for s in fsum)
    scale_b = tuple(lift / s for s in bsum)

    def own_step(i, carry):
        fs, bs, ff, bf = carry[0:4], carry[4:8], carry[8:12], carry[12:16]
        up_to = SPAN - 1 - i
        wf, wb = words[begin + i], words[begin + up_to]
        row, at, none = later(up_to)
        rate_b = jnp.where(none, 0.0, beta[row, at])
        fnew, bnew = [], []
        for t in range(TGT):
            mix = beta[here, i] * fs[t]
            e1, e0 = emission(here, i, t)
            e1, e0 = e1 * ff[t], e0 * ff[t]
            acc = None
            for v in range(TILES):
                x = (fwd[t, v] + mix) * jnp.where((wf & (1 << (2 * v))) != 0, e1, e0)
                fwd[t, v] = x
                fstore[i * TGT + t, v] = x
                acc = x if v == 0 else acc + x
            fnew.append(acc)
        for t in range(TGT):
            mix = rate_b * bs[t]
            e1, e0 = emission(here, up_to, t)
            e1, e0 = e1 * bf[t], e0 * bf[t]
            sums[1, (SPAN - 1 - i) * TGT + t] = bs[t]
            acc = None
            for v in range(TILES):
                b = bwd[t, v] + mix
                bstore[(SPAN - 1 - i) * TGT + t, v] = b
                x = b * jnp.where((wb & (1 << (2 * v))) != 0, e1, e0)
                bwd[t, v] = x
                acc = x if v == 0 else acc + x
            bnew.append(acc)
        fnew = [total(a) for a in fnew]
        bnew = [total(a) for a in bnew]
        for t in range(TGT):
            sums[0, i * TGT + t] = fnew[t]
        one = jnp.ones((8, LANES), jnp.float32)
        return tuple(fnew) + tuple(bnew) + (one,) * 8

    lax.fori_loop(0, SPAN, own_step, tuple(fsum) + tuple(bsum) + scale_f + scale_b, unroll=15)

    def dose(i, carry):
        w = words[begin + i]
        at_row, at, none = later(i)
        kept = jnp.where(none, 1.0, keep[at_row, at])
        for t in range(TGT):
            row = i * TGT + t
            by_f = 1.0 / sums[0, row]
            by_b = kept / sums[1, row]
            num = den = None
            for v in range(TILES):
                f = (fstore[row, v] * by_f).astype(jnp.bfloat16).astype(jnp.float32)
                b = (bstore[row, v] * by_b).astype(jnp.bfloat16).astype(jnp.float32)
                p = f * b
                q = jnp.where((w & (1 << (2 * v))) != 0, p, 0.0)
                num = q if v == 0 else num + q
                den = p if v == 0 else den + p
            nd[0, t, pl.ds(i, 1), :] = jnp.sum(num, axis=0, keepdims=True)
            nd[1, t, pl.ds(i, 1), :] = jnp.sum(den, axis=0, keepdims=True)
        return carry

    lax.fori_loop(0, SPAN, dose, 0, unroll=3)
    line = jnp.ones((8, LANES), jnp.float32)
    which = lax.broadcasted_iota(jnp.int32, (8, 16), 0)
    answer = jnp.zeros((8, 16), jnp.float32)
    for t in range(TGT):
        num, den = [
            lax.dot_general(line, nd[i, t], (((1,), (1,)), ((), ())), precision=lax.Precision.HIGHEST,
                            preferred_element_type=jnp.float32) for i in range(2)]
        answer = jnp.where(which == t, num / den, answer)
    out[...] = answer[0:TGT, 0:SPAN]


def chains(place, beta, keep, for_one, for_zero, sides, own, other, weights_start, weights_end):
    smem = pl.BlockSpec(memory_space=pltpu.SMEM)
    vmem = pl.BlockSpec(memory_space=pltpu.VMEM)
    f32 = jnp.float32
    return pl.pallas_call(
        kernel,
        out_shape=jax.ShapeDtypeStruct((TGT, SPAN), f32),
        in_specs=[smem] * 5 + [vmem] * 3 + [pl.BlockSpec(memory_space=pl.ANY)] * 2,
        out_specs=vmem,
        scratch_shapes=[
            pltpu.VMEM((MARKERS, 8, LANES), jnp.int32),
            pltpu.VMEM((TGT, TILES, 8, LANES), f32),
            pltpu.VMEM((TGT, TILES, 8, LANES), f32),
            pltpu.VMEM((SPAN * TGT, TILES, 8, LANES), f32),
            pltpu.VMEM((SPAN * TGT, TILES, 8, LANES), f32),
            pltpu.VMEM((7, LANES, LANES), f32),
            pltpu.VMEM((2, SPAN * TGT, 8, LANES), f32),
            pltpu.VMEM((24, LANES), f32),
            pltpu.SMEM((24, LANES), f32),
            pltpu.VMEM((2, TGT, 16, LANES), f32),
            pltpu.VMEM((2, TGT, TILES, 8, LANES), f32),
            pltpu.SemaphoreType.DMA,
            pltpu.SemaphoreType.DMA((2,)),
        ],
        compiler_params=pltpu.CompilerParams(vmem_limit_bytes=40 << 20),
    )(place, beta, keep, for_one, for_zero, sides, own, other, weights_start, weights_end)


def local(alleles, observed, map_steps, start_weights, end_weights):
    message = pack(alleles, observed.T, map_steps.reshape(1, SPAN)).reshape(8, 1, 384)
    start, end = [jnp.maximum(x, 0.0) for x in planes(start_weights, end_weights)]
    line = lax.all_to_all(message, "z", 0, 0, tiled=True)
    spread = jnp.broadcast_to(line[:, :, 0:256].reshape(1, 1, 2048), (32, 1, 2048))
    own = lax.all_to_all(spread, ("x", "y"), 0, 0, tiled=True).reshape(512, LANES)
    side = line[:, 0, 256:384]
    swap = [(0, 1), (1, 0)]
    other = lax.ppermute(own, "c", swap)
    partner = lax.ppermute(side, "c", swap)

    core = lax.axis_index("c")
    sides = jnp.concatenate([jnp.where(core == 0, side, partner), jnp.where(core == 0, partner, side)], axis=0)
    rates = 1.0 - jnp.exp(-sides.astype(jnp.float32) / map_unit)
    keep = 1.0 - rates
    beta = (rates / K) / keep
    for_one = jnp.where(sides == 2, 1.0, jnp.where(sides == 1, hit, miss)).astype(jnp.float32)
    for_zero = jnp.where(sides == 2, 1.0, jnp.where(sides == 0, hit, miss)).astype(jnp.float32)
    place = (2 * lax.axis_index("z") + core).astype(jnp.int32).reshape(1)
    return chains(place, beta, keep, for_one, for_zero, sides, own, other, start, end).T


def solution(mesh):
    cut = Mesh(mesh.devices.reshape(8, 2, 4, 8), ("z", "c", "x", "y"))
    grp, hap = ("z", "c"), ("x", "y")
    in_specs = (P(grp, hap), P(grp, hap), P(grp), P(hap, None), P(hap, None))
    return jax.shard_map(local, mesh=cut, in_specs=in_specs, out_specs=P(grp, hap), check_vma=False)
```

```python
import jax
import jax.numpy as jnp
from jax import lax
from jax.experimental import pallas as pl
from jax.experimental.pallas import tpu as pltpu
from jax.sharding import Mesh, PartitionSpec as P

K = 15360
MARKERS = 240
GROUPS = 16
SPAN = 15
TILES = 15
TGT = 4
BLOCKS = MARKERS // 3
LANES = 128
CHUNK = 1920
hit = 0.99
miss = 0.01
map_unit = 100000.0
lift = float(2**60)


def full(value):
    return jnp.broadcast_to(value, (8, LANES))


def total(tile):
    rows = jnp.sum(tile, axis=0, keepdims=True)
    return full(jnp.sum(rows, axis=1, keepdims=True))


def swapped_blocks(tiles, lane):
    tiles = list(tiles)
    for step in (1, 2, 4):
        low = (lane & (16 * step)) == 0
        for j in range(8):
            if j & step:
                continue
            first, second = tiles[j], tiles[j + step]
            tiles[j] = jnp.where(low, first, pltpu.roll(second, 16 * step, 1))
            tiles[j + step] = jnp.where(low, pltpu.roll(first, LANES - 16 * step, 1), second)
    return tiles


def pack_kernel(alleles, observed, steps, message):
    rows = [alleles[m:m + 1, :] for m in range(SPAN)]
    zero = lambda n: jnp.zeros((1, n), jnp.int32)
    first = jnp.concatenate(rows[:8], axis=1)
    second = jnp.concatenate(rows[8:] + [zero(16)], axis=1)
    seen = [observed[t:t + 1, :] for t in range(TGT)]
    third = jnp.concatenate([steps[...], zero(1)] + seen + [zero(52)], axis=1)
    message[...] = jnp.concatenate([first, second, third] * 8, axis=0)


def pack(alleles, observed, steps):
    vmem = pl.BlockSpec(memory_space=pltpu.VMEM)
    return pl.pallas_call(
        pack_kernel, out_shape=jax.ShapeDtypeStruct((24, LANES), jnp.int32),
        in_specs=[vmem] * 3, out_specs=vmem)(alleles, observed, steps)


def planes_kernel(weights_start, weights_end, start, end, stage, tiles):
    lane = lax.broadcasted_iota(jnp.int32, (8, LANES), 1)
    pair_of = []
    for u in range(TILES):
        offset = (LANES * u) % 30 + lane
        pair_of.append(lax.shift_right_logical(offset - 30 * lax.shift_right_logical(offset * 2185, 16), 1))
    for which, weights in enumerate((weights_start, weights_end)):
        for u in range(TILES):
            for s in range(8):
                at = CHUNK * s + LANES * u
                stage[u, 4 * s:4 * s + 4, :] = weights[:, at:at + LANES]
            for t in range(TGT):
                tiles[which * TGT + t, u] = stage[u, pl.ds(t, 8, stride=4), :]
    for p in range(TILES):
        masks = [pair_of[u] == p for u in range(1, TILES)]
        for row in range(2 * TGT):
            chosen = tiles[row, 0]
            for u in range(1, TILES):
                chosen = jnp.where(masks[u - 1], tiles[row, u], chosen)
            if p:
                chosen = pltpu.roll(chosen, LANES - 2 * p, 1)
            if row < TGT:
                start[row, p] = chosen
            else:
                end[row - TGT, p] = chosen


def planes(weights_start, weights_end):
    vmem = pl.BlockSpec(memory_space=pltpu.VMEM)
    laid = jax.ShapeDtypeStruct((TGT, TILES, 8, LANES), jnp.float32)
    return pl.pallas_call(
        planes_kernel,
        out_shape=(laid, laid),
        in_specs=[vmem] * 2, out_specs=(vmem,) * 2,
        scratch_shapes=[pltpu.VMEM((TILES, 32, LANES), jnp.float32), pltpu.VMEM((2 * TGT, TILES, 8, LANES), jnp.float32)],
        cost_estimate=pl.CostEstimate(flops=4_000_000, transcendentals=0, bytes_accessed=1_000_000),
    )(weights_start, weights_end)


def home_of(group):
    return lax.shift_right_logical(group, 1) + 8 * (group & 1)


def emissions_by_block(sides):
    found = []
    values = sides.astype(jnp.float32).astype(jnp.bfloat16)
    block = lax.broadcasted_iota(jnp.int32, (1, LANES), 1)
    group = lax.shift_right_logical(block * 13108, 16)
    within = block - 5 * group
    home = lax.shift_right_logical(group, 1) + 8 * (group & 1)
    mine = lax.broadcasted_iota(jnp.int32, (16, LANES), 0) == home
    source = lax.broadcasted_iota(jnp.int32, (LANES, LANES), 0)
    for q in range(3):
        rows = []
        for t in range(TGT):
            pick = (source == 16 + 15 * t + 3 * within + q).astype(jnp.float32).astype(jnp.bfloat16)
            moved = jnp.dot(values, pick, preferred_element_type=jnp.float32)
            rows.append(jnp.sum(jnp.where(mine, moved, 0.0), axis=0, keepdims=True))
        seen = jnp.concatenate(rows + rows, axis=0)
        found.append(jnp.where(seen == 2.0, 1.0, jnp.where(seen == 1.0, hit, miss)))
        found.append(jnp.where(seen == 2.0, 1.0, jnp.where(seen == 0.0, hit, miss)))
    return found


def kernel(place, beta, keep, for_one, for_zero, sides, own, other, weights_start, weights_end, out,
           words, fwd, bwd, fstore, bstore, counts_in, sums, gv, gs, nd, eb, sem, weight_sems):
    loads = [pltpu.make_async_copy(weights_start, fwd, weight_sems.at[0]),
             pltpu.make_async_copy(weights_end, bwd, weight_sems.at[1])]
    for load in loads:
        load.start()
    group = place[0]
    core = lax.rem(group, 2)
    lane = lax.broadcasted_iota(jnp.int32, (8, LANES), 1)
    half_lane = lax.shift_right_logical(lane, 1)
    odd = lane & 1
    word_at = (47 * half_lane) & 63

    def unpack(z, carry):
        for ref, which in ((own, core), (other, 1 - core)):
            tiles = [ref[pl.ds(16 * q + 2 * z + a, 8, stride=64), :] for a in range(2) for q in range(4)]
            tiles = swapped_blocks(tiles, lane)
            first = (2 * z + which) * SPAN
            for m in range(SPAN):
                picked = jnp.take_along_axis(tiles[m % 8], word_at + (64 if m >= 8 else 0), axis=1)
                words[first + m] = lax.shift_right_logical(picked, odd)
        return carry

    lax.fori_loop(0, 8, unpack, 0, unroll=2)

    def emission(row, m, t):
        at = 16 + 15 * t + m
        return for_one[row, at], for_zero[row, at]

    def count(block, carry):
        w0, w1, w2 = [words[3 * block + j] & 0x15555555 for j in range(3)]
        w01, w12, w02 = w0 & w1, w1 & w2, w0 & w2
        for q, w in enumerate((w0, w1, w2, w01, w12, w02, w01 & w2)):
            ones = lax.population_count(w).astype(jnp.float32)
            counts_in[q, pl.ds(block, 1), :] = jnp.sum(ones, axis=0, keepdims=True)
        return carry

    lax.fori_loop(0, BLOCKS, count, 0, unroll=8)
    ones = jnp.ones((8, LANES), jnp.bfloat16)
    n = []
    for q in range(7):
        table = counts_in[q].astype(jnp.bfloat16)
        n.append(lax.dot_general(ones, table, (((1,), (1,)), ((), ())), preferred_element_type=jnp.float32))
    n0, n1, n2, n01, n12, n02, n012 = n
    a1, a0, b1, b0, c1, c0 = emissions_by_block(sides[...])

    def pair(x1, x0, y1, y0, nx, ny, nxy):
        return nxy * (x1 * y1) + (nx - nxy) * (x1 * y0) + (ny - nxy) * (x0 * y1) + (K - nx - ny + nxy) * (x0 * y0)

    table0 = n0 * a1 + (K - n0) * a0
    table1 = n1 * b1 + (K - n1) * b0
    table2 = n2 * c1 + (K - n2) * c0
    table3 = pair(a1, a0, b1, b0, n0, n1, n01)
    table4 = pair(b1, b0, c1, c0, n1, n2, n12)
    with_a = n012 * (b1 * c1) + (n01 - n012) * (b1 * c0) + (n02 - n012) * (b0 * c1) + (n0 - n01 - n02 + n012) * (b0 * c0)
    rest = (n12 - n012) * (b1 * c1) + (n1 - n01 - n12 + n012) * (b1 * c0) + (n2 - n02 - n12 + n012) * (b0 * c1) \
        + (K - n0 - n1 - n2 + n01 + n12 + n02 - n012) * (b0 * c0)
    table5 = a1 * with_a + a0 * rest
    for i, table in enumerate((table0, table1, table2, table3, table4, table5)):
        gv[TGT * i:TGT * i + TGT, :] = table[0:TGT]
    copy = pltpu.make_async_copy(gv, gs, sem)
    copy.start()

    for load in loads:
        load.wait()

    def sum_of(ref):
        sums_now = []
        for t in range(TGT):
            acc = ref[t, 0]
            for v in range(1, TILES):
                acc = acc + ref[t, v]
            sums_now.append(total(acc))
        return tuple(sums_now)

    def three(state, at, step, carry, reverse, scaled):
        order = (2, 1, 0) if reverse else (0, 1, 2)
        block = 5 * at + step
        row = home_of(at)
        tile_words = [words[3 * block + j] for j in order]
        if reverse:
            if step == 4:
                edge = beta[home_of(jnp.minimum(at + 1, GROUPS - 1)), 0]
                edge = jnp.where(at == GROUPS - 1, 0.0, edge)
            else:
                edge = beta[row, 3 * step + 3]
            rates = [edge, beta[row, 3 * step + 2], beta[row, 3 * step + 1]]
        else:
            rates = [beta[row, 3 * step + j] for j in range(3)]
        singles = order
        pairs = (4, 3) if reverse else (3, 4)
        result = [None] * TGT
        sums_of = {}
        emis = {t: [emission(row, 3 * step + j, t) for j in order] for t in range(TGT)}

        def down(targets):
            accs = {t: [None] * 3 for t in targets}
            first = {t: tuple(e * carry[4 + t] for e in emis[t][0]) if scaled else emis[t][0] for t in targets}
            for v in range(TILES):
                masks = [(w & (1 << (2 * v))) != 0 for w in tile_words]
                for t in targets:
                    y = state[t, v]
                    for j in range(3):
                        e1, e0 = first[t] if j == 0 else emis[t][j]
                        e = jnp.where(masks[j], e1, e0)
                        if j:
                            eb[j - 1, t, v] = e
                        y = y * e
                        accs[t][j] = y if v == 0 else accs[t][j] + y
                    state[t, v] = y
            for t in targets:
                sums_of[t] = [total(a) for a in accs[t]]

        def up(targets):
            mix = {}
            for t in targets:
                q1, q2, q3 = sums_of[t]
                g = lambda q: gs[TGT * q + t, block]
                m0 = rates[0] * (carry[t] * carry[4 + t] if scaled else carry[t])
                s1 = q1 + m0 * g(singles[0])
                m1 = rates[1] * s1
                s2 = (q2 + m0 * g(pairs[0])) + m1 * g(singles[1])
                m2 = rates[2] * s2
                s3 = (q3 + m0 * g(5)) + m1 * g(pairs[1]) + m2 * g(singles[2])
                result[t] = s3
                mix[t] = (m0 * emis[t][0][0] + m1, m0 * emis[t][0][1] + m1, m2)
            for v in range(TILES):
                mask = (tile_words[0] & (1 << (2 * v))) != 0
                for t in targets:
                    h = jnp.where(mask, mix[t][0], mix[t][1])
                    h = h * eb[0, t, v] + mix[t][2]
                    h = h * eb[1, t, v]
                    state[t, v] = state[t, v] + h

        down((0, 1))
        down((2, 3))
        up((0, 1))
        up((2, 3))
        return tuple(result)

    start_sums, end_sums = sum_of(fwd), sum_of(bwd)
    copy.wait()

    def run(state, first, count_groups, reverse, sums_now):
        def one_group(i, sums_now):
            at = first - i if reverse else first + i
            carry = tuple(sums_now) + tuple(lift / s for s in sums_now)
            for j in range(5):
                carry = three(state, at, 4 - j if reverse else j, carry, reverse, j == 0)
            return carry
        return lax.fori_loop(0, count_groups, one_group, sums_now)

    fsum = run(fwd, 0, group, False, start_sums)
    bsum = run(bwd, GROUPS - 1, GROUPS - 1 - group, True, end_sums)

    begin = group * SPAN
    here = home_of(group)
    after = home_of(jnp.minimum(group + 1, GROUPS - 1))

    def later(m):
        last = m == SPAN - 1
        return jnp.where(last, after, here), jnp.where(last, 0, m + 1), jnp.logical_and(last, group == GROUPS - 1)

    scale_f = tuple(lift / s for s in fsum)
    scale_b = tuple(lift / s for s in bsum)

    def own_step(i, carry):
        fs, bs, ff, bf = carry[0:4], carry[4:8], carry[8:12], carry[12:16]
        up_to = SPAN - 1 - i
        wf, wb = words[begin + i], words[begin + up_to]
        row, at, none = later(up_to)
        rate_b = jnp.where(none, 0.0, beta[row, at])
        fnew, bnew = [], []
        for t in range(TGT):
            mix = beta[here, i] * fs[t]
            e1, e0 = emission(here, i, t)
            e1, e0 = e1 * ff[t], e0 * ff[t]
            acc = None
            for v in range(TILES):
                x = (fwd[t, v] + mix) * jnp.where((wf & (1 << (2 * v))) != 0, e1, e0)
                fwd[t, v] = x
                fstore[i * TGT + t, v] = x
                acc = x if v == 0 else acc + x
            fnew.append(acc)
        for t in range(TGT):
            mix = rate_b * bs[t]
            e1, e0 = emission(here, up_to, t)
            e1, e0 = e1 * bf[t], e0 * bf[t]
            sums[1, (SPAN - 1 - i) * TGT + t] = bs[t]
            acc = None
            for v in range(TILES):
                b = bwd[t, v] + mix
                bstore[(SPAN - 1 - i) * TGT + t, v] = b
                x = b * jnp.where((wb & (1 << (2 * v))) != 0, e1, e0)
                bwd[t, v] = x
                acc = x if v == 0 else acc + x
            bnew.append(acc)
        fnew = [total(a) for a in fnew]
        bnew = [total(a) for a in bnew]
        for t in range(TGT):
            sums[0, i * TGT + t] = fnew[t]
        one = jnp.ones((8, LANES), jnp.float32)
        return tuple(fnew) + tuple(bnew) + (one,) * 8

    lax.fori_loop(0, SPAN, own_step, tuple(fsum) + tuple(bsum) + scale_f + scale_b, unroll=15)

    def dose(i, carry):
        w = words[begin + i]
        at_row, at, none = later(i)
        kept = jnp.where(none, 1.0, keep[at_row, at])
        for t in range(TGT):
            row = i * TGT + t
            by_f = 1.0 / sums[0, row]
            by_b = kept / sums[1, row]
            num = den = None
            for v in range(TILES):
                f = (fstore[row, v] * by_f).astype(jnp.bfloat16).astype(jnp.float32)
                b = (bstore[row, v] * by_b).astype(jnp.bfloat16).astype(jnp.float32)
                p = f * b
                q = jnp.where((w & (1 << (2 * v))) != 0, p, 0.0)
                num = q if v == 0 else num + q
                den = p if v == 0 else den + p
            nd[0, t, pl.ds(i, 1), :] = jnp.sum(num, axis=0, keepdims=True)
            nd[1, t, pl.ds(i, 1), :] = jnp.sum(den, axis=0, keepdims=True)
        return carry

    lax.fori_loop(0, SPAN, dose, 0, unroll=3)
    line = jnp.ones((8, LANES), jnp.float32)
    which = lax.broadcasted_iota(jnp.int32, (8, 16), 0)
    answer = jnp.zeros((8, 16), jnp.float32)
    for t in range(TGT):
        num, den = [
            lax.dot_general(line, nd[i, t], (((1,), (1,)), ((), ())), precision=lax.Precision.HIGHEST,
                            preferred_element_type=jnp.float32) for i in range(2)]
        answer = jnp.where(which == t, num / den, answer)
    out[...] = answer[0:TGT, 0:SPAN]


def chains(place, beta, keep, for_one, for_zero, sides, own, other, weights_start, weights_end):
    smem = pl.BlockSpec(memory_space=pltpu.SMEM)
    vmem = pl.BlockSpec(memory_space=pltpu.VMEM)
    f32 = jnp.float32
    return pl.pallas_call(
        kernel,
        out_shape=jax.ShapeDtypeStruct((TGT, SPAN), f32),
        in_specs=[smem] * 5 + [vmem] * 3 + [pl.BlockSpec(memory_space=pl.ANY)] * 2,
        out_specs=vmem,
        scratch_shapes=[
            pltpu.VMEM((MARKERS, 8, LANES), jnp.int32),
            pltpu.VMEM((TGT, TILES, 8, LANES), f32),
            pltpu.VMEM((TGT, TILES, 8, LANES), f32),
            pltpu.VMEM((SPAN * TGT, TILES, 8, LANES), f32),
            pltpu.VMEM((SPAN * TGT, TILES, 8, LANES), f32),
            pltpu.VMEM((7, LANES, LANES), f32),
            pltpu.VMEM((2, SPAN * TGT, 8, LANES), f32),
            pltpu.VMEM((24, LANES), f32),
            pltpu.SMEM((24, LANES), f32),
            pltpu.VMEM((2, TGT, 16, LANES), f32),
            pltpu.VMEM((2, TGT, TILES, 8, LANES), f32),
            pltpu.SemaphoreType.DMA,
            pltpu.SemaphoreType.DMA((2,)),
        ],
        compiler_params=pltpu.CompilerParams(vmem_limit_bytes=40 << 20),
    )(place, beta, keep, for_one, for_zero, sides, own, other, weights_start, weights_end)


def local(alleles, observed, map_steps, start_weights, end_weights):
    message = pack(alleles, observed.T, map_steps.reshape(1, SPAN)).reshape(8, 1, 384)
    start, end = [jnp.maximum(x, 0.0) for x in planes(start_weights, end_weights)]
    line = lax.all_to_all(message, "z", 0, 0, tiled=True)
    spread = jnp.broadcast_to(line[:, :, 0:256].reshape(1, 1, 2048), (32, 1, 2048))
    own = lax.all_to_all(spread, ("x", "y"), 0, 0, tiled=True).reshape(512, LANES)
    side = line[:, 0, 256:384]
    swap = [(0, 1), (1, 0)]
    other = lax.ppermute(own, "c", swap)
    partner = lax.ppermute(side, "c", swap)

    core = lax.axis_index("c")
    sides = jnp.concatenate([jnp.where(core == 0, side, partner), jnp.where(core == 0, partner, side)], axis=0)
    rates = 1.0 - jnp.exp(-sides.astype(jnp.float32) / map_unit)
    keep = 1.0 - rates
    beta = (rates / K) / keep
    for_one = jnp.where(sides == 2, 1.0, jnp.where(sides == 1, hit, miss)).astype(jnp.float32)
    for_zero = jnp.where(sides == 2, 1.0, jnp.where(sides == 0, hit, miss)).astype(jnp.float32)
    place = (2 * lax.axis_index("z") + core).astype(jnp.int32).reshape(1)
    return chains(place, beta, keep, for_one, for_zero, sides, own, other, start, end).T


def solution(mesh):
    cut = Mesh(mesh.devices.reshape(8, 2, 4, 8), ("z", "c", "x", "y"))
    grp, hap = ("z", "c"), ("x", "y")
    in_specs = (P(grp, hap), P(grp, hap), P(grp), P(hap, None), P(hap, None))
    return jax.shard_map(local, mesh=cut, in_specs=in_specs, out_specs=P(grp, hap), check_vma=False)
```

```python
import jax
import jax.numpy as jnp
from jax import lax
from jax.experimental import pallas as pl
from jax.experimental.pallas import tpu as pltpu
from jax.sharding import Mesh, PartitionSpec as P

K = 15360
MARKERS = 240
GROUPS = 16
SPAN = 15
TILES = 15
TGT = 4
BLOCKS = MARKERS // 3
LANES = 128
CHUNK = 1920
hit = 0.99
miss = 0.01
map_unit = 100000.0
lift = float(2**60)


def full(value):
    return jnp.broadcast_to(value, (8, LANES))


def total(tile):
    rows = jnp.sum(tile, axis=0, keepdims=True)
    return full(jnp.sum(rows, axis=1, keepdims=True))


def swapped_blocks(tiles, lane):
    tiles = list(tiles)
    for step in (1, 2, 4):
        low = (lane & (16 * step)) == 0
        for j in range(8):
            if j & step:
                continue
            first, second = tiles[j], tiles[j + step]
            tiles[j] = jnp.where(low, first, pltpu.roll(second, 16 * step, 1))
            tiles[j + step] = jnp.where(low, pltpu.roll(first, LANES - 16 * step, 1), second)
    return tiles


def pack_kernel(alleles, observed, steps, message):
    rows = [alleles[m:m + 1, :] for m in range(SPAN)]
    zero = lambda n: jnp.zeros((1, n), jnp.int32)
    first = jnp.concatenate(rows[:8], axis=1)
    second = jnp.concatenate(rows[8:] + [zero(16)], axis=1)
    seen = [observed[t:t + 1, :] for t in range(TGT)]
    third = jnp.concatenate([steps[...], zero(1)] + seen + [zero(52)], axis=1)
    message[...] = jnp.concatenate([first, second, third] * 8, axis=0)


def pack(alleles, observed, steps):
    vmem = pl.BlockSpec(memory_space=pltpu.VMEM)
    return pl.pallas_call(
        pack_kernel, out_shape=jax.ShapeDtypeStruct((24, LANES), jnp.int32),
        in_specs=[vmem] * 3, out_specs=vmem)(alleles, observed, steps)


def planes_kernel(weights_start, weights_end, start, end, stage, tiles):
    lane = lax.broadcasted_iota(jnp.int32, (8, LANES), 1)
    pair_of = []
    for u in range(TILES):
        offset = (LANES * u) % 30 + lane
        pair_of.append(lax.shift_right_logical(offset - 30 * lax.shift_right_logical(offset * 2185, 16), 1))
    for which, weights in enumerate((weights_start, weights_end)):
        for u in range(TILES):
            for s in range(8):
                at = CHUNK * s + LANES * u
                stage[u, 4 * s:4 * s + 4, :] = weights[:, at:at + LANES]
            for t in range(TGT):
                tiles[which * TGT + t, u] = stage[u, pl.ds(t, 8, stride=4), :]
    for p in range(TILES):
        masks = [pair_of[u] == p for u in range(1, TILES)]
        for row in range(2 * TGT):
            chosen = tiles[row, 0]
            for u in range(1, TILES):
                chosen = jnp.where(masks[u - 1], tiles[row, u], chosen)
            if p:
                chosen = pltpu.roll(chosen, LANES - 2 * p, 1)
            if row < TGT:
                start[row, p] = chosen
            else:
                end[row - TGT, p] = chosen


def planes(weights_start, weights_end):
    vmem = pl.BlockSpec(memory_space=pltpu.VMEM)
    laid = jax.ShapeDtypeStruct((TGT, TILES, 8, LANES), jnp.float32)
    return pl.pallas_call(
        planes_kernel,
        out_shape=(laid, laid),
        in_specs=[vmem] * 2, out_specs=(vmem,) * 2,
        scratch_shapes=[pltpu.VMEM((TILES, 32, LANES), jnp.float32), pltpu.VMEM((2 * TGT, TILES, 8, LANES), jnp.float32)],
        cost_estimate=pl.CostEstimate(flops=4_000_000, transcendentals=0, bytes_accessed=1_000_000),
    )(weights_start, weights_end)


def home_of(group):
    return lax.shift_right_logical(group, 1) + 8 * (group & 1)


def emissions_by_block(sides):
    found = []
    values = sides.astype(jnp.float32).astype(jnp.bfloat16)
    block = lax.broadcasted_iota(jnp.int32, (1, LANES), 1)
    group = lax.shift_right_logical(block * 13108, 16)
    within = block - 5 * group
    home = lax.shift_right_logical(group, 1) + 8 * (group & 1)
    mine = lax.broadcasted_iota(jnp.int32, (16, LANES), 0) == home
    source = lax.broadcasted_iota(jnp.int32, (LANES, LANES), 0)
    for q in range(3):
        rows = []
        for t in range(TGT):
            pick = (source == 16 + 15 * t + 3 * within + q).astype(jnp.float32).astype(jnp.bfloat16)
            moved = jnp.dot(values, pick, preferred_element_type=jnp.float32)
            rows.append(jnp.sum(jnp.where(mine, moved, 0.0), axis=0, keepdims=True))
        seen = jnp.concatenate(rows + rows, axis=0)
        found.append(jnp.where(seen == 2.0, 1.0, jnp.where(seen == 1.0, hit, miss)))
        found.append(jnp.where(seen == 2.0, 1.0, jnp.where(seen == 0.0, hit, miss)))
    return found


def kernel(place, beta, keep, for_one, for_zero, sides, own, other, weights_start, weights_end, out,
           words, fwd, bwd, fstore, bstore, counts_in, sums, gv, gs, nd, eb, sem, weight_sems):
    loads = [pltpu.make_async_copy(weights_start, fwd, weight_sems.at[0]),
             pltpu.make_async_copy(weights_end, bwd, weight_sems.at[1])]
    for load in loads:
        load.start()
    group = place[0]
    core = lax.rem(group, 2)
    lane = lax.broadcasted_iota(jnp.int32, (8, LANES), 1)
    half_lane = lax.shift_right_logical(lane, 1)
    odd = lane & 1
    word_at = (47 * half_lane) & 63

    def unpack(z, carry):
        for ref, which in ((own, core), (other, 1 - core)):
            tiles = [ref[pl.ds(16 * q + 2 * z + a, 8, stride=64), :] for a in range(2) for q in range(4)]
            tiles = swapped_blocks(tiles, lane)
            first = (2 * z + which) * SPAN
            for m in range(SPAN):
                picked = jnp.take_along_axis(tiles[m % 8], word_at + (64 if m >= 8 else 0), axis=1)
                words[first + m] = lax.shift_right_logical(picked, odd)
        return carry

    lax.fori_loop(0, 8, unpack, 0)

    def emission(row, m, t):
        at = 16 + 15 * t + m
        return for_one[row, at], for_zero[row, at]

    def count(block, carry):
        w0, w1, w2 = [words[3 * block + j] & 0x15555555 for j in range(3)]
        w01, w12, w02 = w0 & w1, w1 & w2, w0 & w2
        for q, w in enumerate((w0, w1, w2, w01, w12, w02, w01 & w2)):
            ones = lax.population_count(w).astype(jnp.float32)
            counts_in[q, pl.ds(block, 1), :] = jnp.sum(ones, axis=0, keepdims=True)
        return carry

    lax.fori_loop(0, BLOCKS, count, 0, unroll=8)
    ones = jnp.ones((8, LANES), jnp.bfloat16)
    n = []
    for q in range(7):
        table = counts_in[q].astype(jnp.bfloat16)
        n.append(lax.dot_general(ones, table, (((1,), (1,)), ((), ())), preferred_element_type=jnp.float32))
    n0, n1, n2, n01, n12, n02, n012 = n
    a1, a0, b1, b0, c1, c0 = emissions_by_block(sides[...])

    def pair(x1, x0, y1, y0, nx, ny, nxy):
        return nxy * (x1 * y1) + (nx - nxy) * (x1 * y0) + (ny - nxy) * (x0 * y1) + (K - nx - ny + nxy) * (x0 * y0)

    table0 = n0 * a1 + (K - n0) * a0
    table1 = n1 * b1 + (K - n1) * b0
    table2 = n2 * c1 + (K - n2) * c0
    table3 = pair(a1, a0, b1, b0, n0, n1, n01)
    table4 = pair(b1, b0, c1, c0, n1, n2, n12)
    with_a = n012 * (b1 * c1) + (n01 - n012) * (b1 * c0) + (n02 - n012) * (b0 * c1) + (n0 - n01 - n02 + n012) * (b0 * c0)
    rest = (n12 - n012) * (b1 * c1) + (n1 - n01 - n12 + n012) * (b1 * c0) + (n2 - n02 - n12 + n012) * (b0 * c1) \
        + (K - n0 - n1 - n2 + n01 + n12 + n02 - n012) * (b0 * c0)
    table5 = a1 * with_a + a0 * rest
    for i, table in enumerate((table0, table1, table2, table3, table4, table5)):
        gv[TGT * i:TGT * i + TGT, :] = table[0:TGT]
    copy = pltpu.make_async_copy(gv, gs, sem)
    copy.start()

    for load in loads:
        load.wait()

    def sum_of(ref):
        sums_now = []
        for t in range(TGT):
            acc = ref[t, 0]
            for v in range(1, TILES):
                acc = acc + ref[t, v]
            sums_now.append(total(acc))
        return tuple(sums_now)

    def three(state, at, step, carry, reverse, scaled):
        order = (2, 1, 0) if reverse else (0, 1, 2)
        block = 5 * at + step
        row = home_of(at)
        tile_words = [words[3 * block + j] for j in order]
        if reverse:
            if step == 4:
                edge = beta[home_of(jnp.minimum(at + 1, GROUPS - 1)), 0]
                edge = jnp.where(at == GROUPS - 1, 0.0, edge)
            else:
                edge = beta[row, 3 * step + 3]
            rates = [edge, beta[row, 3 * step + 2], beta[row, 3 * step + 1]]
        else:
            rates = [beta[row, 3 * step + j] for j in range(3)]
        singles = order
        pairs = (4, 3) if reverse else (3, 4)
        result = [None] * TGT
        sums_of = {}
        emis = {t: [emission(row, 3 * step + j, t) for j in order] for t in range(TGT)}

        def down(targets):
            accs = {t: [None] * 3 for t in targets}
            first = {t: tuple(e * carry[4 + t] for e in emis[t][0]) if scaled else emis[t][0] for t in targets}
            for v in range(TILES):
                masks = [(w & (1 << (2 * v))) != 0 for w in tile_words]
                for t in targets:
                    y = state[t, v]
                    for j in range(3):
                        e1, e0 = first[t] if j == 0 else emis[t][j]
                        e = jnp.where(masks[j], e1, e0)
                        if j:
                            eb[j - 1, t, v] = e
                        y = y * e
                        accs[t][j] = y if v == 0 else accs[t][j] + y
                    state[t, v] = y
            for t in targets:
                sums_of[t] = [total(a) for a in accs[t]]

        def up(targets):
            mix = {}
            for t in targets:
                q1, q2, q3 = sums_of[t]
                g = lambda q: gs[TGT * q + t, block]
                m0 = rates[0] * (carry[t] * carry[4 + t] if scaled else carry[t])
                s1 = q1 + m0 * g(singles[0])
                m1 = rates[1] * s1
                s2 = (q2 + m0 * g(pairs[0])) + m1 * g(singles[1])
                m2 = rates[2] * s2
                s3 = (q3 + m0 * g(5)) + m1 * g(pairs[1]) + m2 * g(singles[2])
                result[t] = s3
                mix[t] = (m0 * emis[t][0][0] + m1, m0 * emis[t][0][1] + m1, m2)
            for v in range(TILES):
                mask = (tile_words[0] & (1 << (2 * v))) != 0
                for t in targets:
                    h = jnp.where(mask, mix[t][0], mix[t][1])
                    h = h * eb[0, t, v] + mix[t][2]
                    h = h * eb[1, t, v]
                    state[t, v] = state[t, v] + h

        down((0, 1))
        down((2, 3))
        up((0, 1))
        up((2, 3))
        return tuple(result)

    start_sums, end_sums = sum_of(fwd), sum_of(bwd)
    copy.wait()

    def run(state, first, count_groups, reverse, sums_now):
        def one_group(i, sums_now):
            at = first - i if reverse else first + i
            carry = tuple(sums_now) + tuple(lift / s for s in sums_now)
            for j in range(5):
                carry = three(state, at, 4 - j if reverse else j, carry, reverse, j == 0)
            return carry
        return lax.fori_loop(0, count_groups, one_group, sums_now)

    fsum = run(fwd, 0, group, False, start_sums)
    bsum = run(bwd, GROUPS - 1, GROUPS - 1 - group, True, end_sums)

    begin = group * SPAN
    here = home_of(group)
    after = home_of(jnp.minimum(group + 1, GROUPS - 1))

    def later(m):
        last = m == SPAN - 1
        return jnp.where(last, after, here), jnp.where(last, 0, m + 1), jnp.logical_and(last, group == GROUPS - 1)

    scale_f = tuple(lift / s for s in fsum)
    scale_b = tuple(lift / s for s in bsum)

    def own_step(i, carry):
        fs, bs, ff, bf = carry[0:4], carry[4:8], carry[8:12], carry[12:16]
        up_to = SPAN - 1 - i
        wf, wb = words[begin + i], words[begin + up_to]
        row, at, none = later(up_to)
        rate_b = jnp.where(none, 0.0, beta[row, at])
        fnew, bnew = [], []
        for t in range(TGT):
            mix = beta[here, i] * fs[t]
            e1, e0 = emission(here, i, t)
            e1, e0 = e1 * ff[t], e0 * ff[t]
            acc = None
            for v in range(TILES):
                x = (fwd[t, v] + mix) * jnp.where((wf & (1 << (2 * v))) != 0, e1, e0)
                fwd[t, v] = x
                fstore[i * TGT + t, v] = x
                acc = x if v == 0 else acc + x
            fnew.append(acc)
        for t in range(TGT):
            mix = rate_b * bs[t]
            e1, e0 = emission(here, up_to, t)
            e1, e0 = e1 * bf[t], e0 * bf[t]
            sums[1, (SPAN - 1 - i) * TGT + t] = bs[t]
            acc = None
            for v in range(TILES):
                b = bwd[t, v] + mix
                bstore[(SPAN - 1 - i) * TGT + t, v] = b
                x = b * jnp.where((wb & (1 << (2 * v))) != 0, e1, e0)
                bwd[t, v] = x
                acc = x if v == 0 else acc + x
            bnew.append(acc)
        fnew = [total(a) for a in fnew]
        bnew = [total(a) for a in bnew]
        for t in range(TGT):
            sums[0, i * TGT + t] = fnew[t]
        one = jnp.ones((8, LANES), jnp.float32)
        return tuple(fnew) + tuple(bnew) + (one,) * 8

    lax.fori_loop(0, SPAN, own_step, tuple(fsum) + tuple(bsum) + scale_f + scale_b, unroll=15)

    def dose(i, carry):
        w = words[begin + i]
        at_row, at, none = later(i)
        kept = jnp.where(none, 1.0, keep[at_row, at])
        for t in range(TGT):
            row = i * TGT + t
            by_f = 1.0 / sums[0, row]
            by_b = kept / sums[1, row]
            num = den = None
            for v in range(TILES):
                f = (fstore[row, v] * by_f).astype(jnp.bfloat16).astype(jnp.float32)
                b = (bstore[row, v] * by_b).astype(jnp.bfloat16).astype(jnp.float32)
                p = f * b
                q = jnp.where((w & (1 << (2 * v))) != 0, p, 0.0)
                num = q if v == 0 else num + q
                den = p if v == 0 else den + p
            nd[0, t, pl.ds(i, 1), :] = jnp.sum(num, axis=0, keepdims=True)
            nd[1, t, pl.ds(i, 1), :] = jnp.sum(den, axis=0, keepdims=True)
        return carry

    lax.fori_loop(0, SPAN, dose, 0, unroll=3)
    line = jnp.ones((8, LANES), jnp.float32)
    which = lax.broadcasted_iota(jnp.int32, (8, 16), 0)
    answer = jnp.zeros((8, 16), jnp.float32)
    for t in range(TGT):
        num, den = [
            lax.dot_general(line, nd[i, t], (((1,), (1,)), ((), ())), precision=lax.Precision.HIGHEST,
                            preferred_element_type=jnp.float32) for i in range(2)]
        answer = jnp.where(which == t, num / den, answer)
    out[...] = answer[0:TGT, 0:SPAN]


def chains(place, beta, keep, for_one, for_zero, sides, own, other, weights_start, weights_end):
    smem = pl.BlockSpec(memory_space=pltpu.SMEM)
    vmem = pl.BlockSpec(memory_space=pltpu.VMEM)
    f32 = jnp.float32
    return pl.pallas_call(
        kernel,
        out_shape=jax.ShapeDtypeStruct((TGT, SPAN), f32),
        in_specs=[smem] * 5 + [vmem] * 3 + [pl.BlockSpec(memory_space=pl.ANY)] * 2,
        out_specs=vmem,
        scratch_shapes=[
            pltpu.VMEM((MARKERS, 8, LANES), jnp.int32),
            pltpu.VMEM((TGT, TILES, 8, LANES), f32),
            pltpu.VMEM((TGT, TILES, 8, LANES), f32),
            pltpu.VMEM((SPAN * TGT, TILES, 8, LANES), f32),
            pltpu.VMEM((SPAN * TGT, TILES, 8, LANES), f32),
            pltpu.VMEM((7, LANES, LANES), f32),
            pltpu.VMEM((2, SPAN * TGT, 8, LANES), f32),
            pltpu.VMEM((24, LANES), f32),
            pltpu.SMEM((24, LANES), f32),
            pltpu.VMEM((2, TGT, 16, LANES), f32),
            pltpu.VMEM((2, TGT, TILES, 8, LANES), f32),
            pltpu.SemaphoreType.DMA,
            pltpu.SemaphoreType.DMA((2,)),
        ],
        compiler_params=pltpu.CompilerParams(vmem_limit_bytes=40 << 20),
    )(place, beta, keep, for_one, for_zero, sides, own, other, weights_start, weights_end)


def local(alleles, observed, map_steps, start_weights, end_weights):
    message = pack(alleles, observed.T, map_steps.reshape(1, SPAN)).reshape(8, 1, 384)
    start, end = [jnp.maximum(x, 0.0) for x in planes(start_weights, end_weights)]
    line = lax.all_to_all(message, "z", 0, 0, tiled=True)
    spread = jnp.broadcast_to(line[:, :, 0:256].reshape(1, 1, 2048), (32, 1, 2048))
    own = lax.all_to_all(spread, ("x", "y"), 0, 0, tiled=True).reshape(512, LANES)
    side = line[:, 0, 256:384]
    swap = [(0, 1), (1, 0)]
    other = lax.ppermute(own, "c", swap)
    partner = lax.ppermute(side, "c", swap)

    core = lax.axis_index("c")
    sides = jnp.concatenate([jnp.where(core == 0, side, partner), jnp.where(core == 0, partner, side)], axis=0)
    rates = 1.0 - jnp.exp(-sides.astype(jnp.float32) / map_unit)
    keep = 1.0 - rates
    beta = (rates / K) / keep
    for_one = jnp.where(sides == 2, 1.0, jnp.where(sides == 1, hit, miss)).astype(jnp.float32)
    for_zero = jnp.where(sides == 2, 1.0, jnp.where(sides == 0, hit, miss)).astype(jnp.float32)
    place = (2 * lax.axis_index("z") + core).astype(jnp.int32).reshape(1)
    return chains(place, beta, keep, for_one, for_zero, sides, own, other, start, end).T


def solution(mesh):
    cut = Mesh(mesh.devices.reshape(8, 2, 4, 8), ("z", "c", "x", "y"))
    grp, hap = ("z", "c"), ("x", "y")
    in_specs = (P(grp, hap), P(grp, hap), P(grp), P(hap, None), P(hap, None))
    return jax.shard_map(local, mesh=cut, in_specs=in_specs, out_specs=P(grp, hap), check_vma=False)
```
